256 devices in a mesh: energy: 32 (over x_lo, z, core), mom: 8 (over x_hi, y).
Axes of the slice: x: 4 (x_hi: 2, x_lo: 2; x = x_hi * 2 + x_lo), y: 4, z: 8, core: 2. Of those that a mesh axis runs over, the one named last changes fastest.
Arguments:
- sigma_in: float32 [128, 8, 2, 256, 256], P('energy', 'mom'), may hold values from -0.1875 to 0.1875
- hamiltonian: float32 [8, 2, 256, 256], P('mom'), may hold values from -0.375 to 0.375
- coupling: float32 [8, 256, 256], P('mom'), may hold values from -0.1875 to 0.1875
- energies: float32 [128], replicated, may hold values from 1.4 to 2, as said below
- counts: int32 [128], replicated, may hold values from 2 to 4, as said below
- strengths: float32 [16], replicated, may hold values from 0.05625 to 0.1875
- offsets: int32 [16], replicated, may hold values from 0 to 7
Outputs:
- sigma_next: float32 [128, 8, 2, 256, 256], P('energy', 'mom')
The draws below stay inside these ranges and needn't reach their ends.
Inputs may be any that keep to these rules, and one draw needn't show every extreme that they name: `energies`: increasing along the grid. `counts`: each point needs either 2 or 4 sweeps, and some point needs 4.
All inputs are finite; a program needn't handle non-finite values.
Results may differ from the reference program's by a relative error of at most 0.0003.
Values sent between devices are 32-bit elements; how exact they have to be, the bound alone decides.
No kernel may reach another device: no remote copies, remote signals or barrier semaphores. Data moves between devices by JAX's collectives and lax.ppermute only.
A program may use at most 64 MiB of HBM per device.

```python
import math
import jax
import jax.numpy as jnp
from jax import lax

M = 256
E_DEV = 4
S_LO = 2
S_MAX = 4
NQ = 16
E_TOT = 128
K = 8
N_ENERGY = 32
N_MOM = 8


def draw_energies(key, part):
    key_gaps, key_block = jax.random.split(jax.random.fold_in(key, 3))
    blocks = E_TOT // E_DEV
    wide_gap = min(0.03, 0.24 / E_DEV)
    planted = jax.random.randint(key_block, (), 0, blocks)
    gap_index = jnp.arange(E_TOT - 1, dtype=jnp.int32)
    inside = (gap_index >= planted * E_DEV) & (gap_index < planted * E_DEV + E_DEV - 1)
    raw_gaps = jax.random.uniform(key_gaps, (E_TOT - 1,), jnp.float32, 0.3, 1.0)
    raw_gaps = jnp.where(inside, 0.0, raw_gaps)
    remaining = 0.58 - wide_gap * (E_DEV - 1)
    gaps = jnp.where(inside, wide_gap, raw_gaps * (remaining / jnp.sum(raw_gaps)))
    steps_taken = jnp.concatenate([jnp.zeros((1,), jnp.float32), jnp.cumsum(gaps)])
    return 1.405 + steps_taken


def draw_counts(key, part):
    key_slow, key_place = jax.random.split(jax.random.fold_in(key, 7))
    index = jnp.arange(E_TOT, dtype=jnp.int32)
    low_band = max(E_TOT // 4, 1)
    chance = jnp.where(index < low_band, 10, 1)
    rolled = jax.random.randint(key_slow, (E_TOT,), 0, 20)
    forced = jax.random.randint(key_place, (), 0, low_band)
    slowed = (rolled < chance) | (index == forced)
    return jnp.where(slowed, S_MAX, S_LO).astype(jnp.int32)


def with_ends(drawn, key, smallest, top_value):
    spot = [jax.random.randint(jax.random.fold_in(key, axis), (), 0, length) for axis, length in enumerate(drawn.shape)]
    longest = drawn.shape.index(max(drawn.shape))
    beside = spot[:longest] + [(spot[longest] + 1) % drawn.shape[longest]] + spot[longest + 1:]
    return drawn.at[tuple(spot)].set(smallest).at[tuple(beside)].set(top_value)


def level_of(rng, dims, shards, low, largest):
    gain, own = 1.0, jax.random.fold_in(rng, 6)
    for dim, blocks in shards:
        draws = jnp.exp(jax.random.uniform(jax.random.fold_in(own, dim), (blocks,), jnp.float32, low / len(shards), largest / len(shards)))
        gain = gain * jnp.repeat(draws, dims[dim] // blocks).reshape([-1 if axis == dim else 1 for axis in range(len(dims))])
    return gain


def normal_values(rng, dims, spread, most, shards=(), kind=jnp.bfloat16):
    values = jax.random.normal(rng, dims, jnp.float32) * spread
    if len(shards) > 0:
        values = level_of(rng, dims, shards, -0.22, 0.18) * values
    return jnp.clip(values, min=-most, max=most).astype(kind)


def setup_inputs(seed: int = 0) -> dict:
    seeds = jax.random.split(jax.random.key(seed), 8)
    sigma_in = normal_values(seeds[0], (E_TOT, K, 2, M, M), (4 * M) ** -0.5, 0.1875, ((0, 32), (1, 8)), jnp.float32)
    hamiltonian = normal_values(seeds[1], (K, 2, M, M), M ** -0.5, 0.375, ((0, 8),), jnp.float32)
    coupling = normal_values(seeds[2], (K, M, M), (4 * M) ** -0.5, 0.1875, ((0, 8),), jnp.float32)
    energies = draw_energies(jax.random.fold_in(seeds[7], 71), 0)
    counts = draw_counts(jax.random.fold_in(seeds[7], 71), 0)
    strengths = jnp.clip(jnp.exp(jax.random.uniform(seeds[5], (NQ,), jnp.float32, math.log(0.05625), math.log(0.1875))), 0.05625, 0.1875)
    offsets = with_ends(jax.random.randint(seeds[6], (NQ,), 0, N_MOM), jax.random.fold_in(seeds[6], 1), 0, N_MOM - 1).astype(jnp.int32)
    return dict(sigma_in=sigma_in, hamiltonian=hamiltonian, coupling=coupling, energies=energies, counts=counts, strengths=strengths, offsets=offsets)


PRECISE = lax.Precision.HIGHEST
MIX_RATE = 0.6
PHONON = 0.1
BROADENING = 0.02


def product(left_side, right_side):
    return jnp.dot(left_side, right_side, precision=PRECISE, preferred_element_type=jnp.float32)


def invert(matrix, energy, sweeps):
    identity = jnp.eye(matrix.shape[0], dtype=jnp.float32)
    estimate = identity / energy
    for sweep_index in range(S_MAX):
        updated = 2.0 * estimate - product(estimate, product(matrix, estimate))
        estimate = jnp.where(sweep_index < sweeps, updated, estimate)
    return estimate


def solve_point(ham_block, coupling_block, sigma_pair, energy, sweeps):
    identity = jnp.eye(ham_block.shape[1], dtype=jnp.float32)
    left_matrix = energy * identity - ham_block[0] - sigma_pair[0]
    left_inverse = invert(left_matrix, energy, sweeps)
    inverse_coupled = product(left_inverse, coupling_block)
    coupled_inverse = product(coupling_block.T, left_inverse)
    right_matrix = energy * identity - ham_block[1] - sigma_pair[1] - product(coupling_block.T, inverse_coupled)
    right_green = invert(right_matrix, energy, sweeps)
    left_green = left_inverse + product(product(inverse_coupled, right_green), coupled_inverse)
    return jnp.stack([left_green, right_green])


def lorentz(offset):
    scaled = offset / BROADENING
    return 1.0 / (1.0 + scaled * scaled)


def build_kernel(row_energy, column_energy):
    spacing = row_energy[:, None] - column_energy[None, :]
    kernel = lorentz(spacing - PHONON) + lorentz(spacing + PHONON)
    return kernel / jnp.sum(kernel, axis=1, keepdims=True)


def reference(sigma_in, hamiltonian, coupling, energies, counts, strengths, offsets):
    def per_energy(held_point):
        sigma_row, energy, sweeps = held_point

        def per_momentum(ham_block, coupling_block, sigma_pair):
            return solve_point(ham_block, coupling_block, sigma_pair, energy, sweeps)

        return jax.vmap(per_momentum)(hamiltonian, coupling, sigma_row)

    green_blocks = lax.map(per_energy, (sigma_in, energies, counts))
    shift_index = jnp.arange(K, dtype=jnp.int32)
    weights = jnp.sum(strengths[:, None] * (offsets[:, None] == shift_index[None, :]).astype(jnp.float32), axis=0)
    kernel = build_kernel(energies, energies)
    piece_width = 2 * M * M // N_ENERGY
    flattened = green_blocks.reshape(E_TOT, K, 2 * M * M)

    def per_block(block_index):
        element_block = lax.dynamic_slice_in_dim(flattened, block_index * piece_width, piece_width, 2)
        mixed_sum = weights[0] * element_block
        for offset_step in range(1, K):
            mixed_sum = mixed_sum + weights[offset_step] * jnp.roll(element_block, offset_step, axis=1)
        return jnp.einsum("ae,ekf->akf", kernel, mixed_sum, precision=PRECISE)

    pieces = lax.map(per_block, jnp.arange(N_ENERGY, dtype=jnp.int32))
    sigma_new = jnp.transpose(pieces, (1, 2, 0, 3)).reshape(sigma_in.shape)
    return (1.0 - MIX_RATE) * sigma_in + MIX_RATE * sigma_new
```

```python
import functools

import jax
import jax.numpy as jnp
from jax import lax
from jax.experimental import pallas as pl
from jax.experimental.pallas import tpu as pltpu
from jax.sharding import Mesh
from jax.sharding import PartitionSpec as P

MIX_RATE = 0.6
PHONON = 0.1
BROADENING = 0.02

M = 256
PTS = 4
ZN = 8
WN = 32
KN = 8
E4 = 4
SLAB = 2 * M // ZN
PLANE = ("xl", "c", "xh", "y")
F32 = jnp.float32
BF16 = jnp.bfloat16
LIMIT = 48 * 1024 * 1024


def vmem():
    return pl.BlockSpec(memory_space=pltpu.VMEM)


def smem():
    return pl.BlockSpec(memory_space=pltpu.SMEM)


def split(x):
    high = x.astype(BF16)
    return high, (x - high.astype(F32)).astype(BF16)


def dot3(a, b):
    left = jnp.concatenate([a[0], a[0], a[1]], axis=1)
    right = jnp.concatenate([b[0], b[1], b[0]], axis=0)
    return jnp.dot(left, right, preferred_element_type=F32)


def both(top, bottom):
    return tuple(jnp.concatenate([t, b], axis=0) for t, b in zip(top, bottom))


def invert_pair(residuals, scales, slow, estimate_ref):
    rows = lax.broadcasted_iota(jnp.int32, (M, M), 0)
    cols = lax.broadcasted_iota(jnp.int32, (M, M), 1)
    eye = (rows == cols).astype(F32)
    estimates, squares = [], []
    for i in range(2):
        pair = split(residuals[i])
        squares.append(dot3(pair, pair))
    square_pairs = [split(s) for s in squares]
    for i in range(2):
        first = (eye + residuals[i]) * scales[i]
        second = first + dot3(split(first), square_pairs[i])
        estimate_ref[i] = second

    @pl.when(slow[0] | slow[1])
    def _():
        fourths = [dot3(square_pairs[i], square_pairs[i]) for i in range(2)]
        for i in range(2):
            fourth = split(fourths[i])
            second = estimate_ref[i]
            stacked = dot3(both(split(second), fourth), fourth)
            third = second + stacked[:M]
            last = third + dot3(split(third), split(stacked[M:]))
            estimate_ref[i] = jnp.where(slow[i], last, second)


def swap_halves(x, y):
    low = lax.broadcasted_iota(jnp.int32, x.shape, x.ndim - 2) < 4
    axis = x.ndim - 2
    first = jnp.where(low, x, pltpu.roll(y, 4, axis))
    second = jnp.where(low, pltpu.roll(x, 4, axis), y)
    return first, second


def solve_kernel(pair, by_shift, sigma_ref, ham_ref, coup_ref, energy_ref, count_ref, *rest):
    outs, (left_ref, right_ref, green_ref) = rest[:-3], rest[-3:]
    z = lax.axis_index("z")
    rank = (lax.axis_index("xl") * ZN + z) * 2 + lax.axis_index("c")
    base = rank * PTS + 2 * pair
    energy = [energy_ref[base + i] for i in range(2)]
    slow = [count_ref[base + i] > 2 for i in range(2)]
    scale = [1.0 / jnp.full((M, M), energy[i], F32) for i in range(2)]
    coupling = split(coup_ref[...])
    turned = split(coup_ref[...].T)
    residual = [(ham_ref[:M] + sigma_ref[i, :M]) * scale[i] for i in range(2)]
    invert_pair(residual, scale, slow, left_ref)
    inverse = [split(left_ref[i]) for i in range(2)]
    coupled = [split(dot3(inverse[i], coupling)) for i in range(2)]
    residual = [
        (ham_ref[M:] + sigma_ref[i, M:] + dot3(turned, coupled[i])) * scale[i] for i in range(2)
    ]
    invert_pair(residual, scale, slow, right_ref)
    for i in range(2):
        right = right_ref[i]
        green_ref[i, M:] = right
        back = split(dot3(turned, inverse[i]))
        through = split(dot3(coupled[i], split(right)))
        green_ref[i, :M] = left_ref[i] + dot3(through, back)
    for d in range(ZN):
        slab = pl.ds(pl.multiple_of(lax.rem(z + d, ZN) * SLAB, SLAB), SLAB)
        first = green_ref[0, slab].reshape(SLAB // 8, 8, M)
        second = green_ref[1, slab].reshape(SLAB // 8, 8, M)
        for parity, tiles in enumerate(swap_halves(first, second)):
            for half in range(2):
                part = tiles[:, :, half * 128 : half * 128 + 128]
                for t in range(SLAB // 8):
                    w = 4 * t + 2 * parity + half
                    if by_shift:
                        outs[d][w] = part[t]
                    else:
                        outs[0][w, d] = part[t]


def solve(pair, by_shift, sigma, ham, coupling, energies, counts):
    if by_shift:
        shape = [jax.ShapeDtypeStruct((WN, 8, 128), F32)] * ZN
        specs = [pl.BlockSpec((WN, 8, 128), lambda i: (0, 0, 0))] * ZN
    else:
        shape = [jax.ShapeDtypeStruct((WN, ZN, 8, 128), F32)]
        specs = [pl.BlockSpec((WN, ZN, 8, 128), lambda i: (0, 0, 0, 0))]
    return pl.pallas_call(
        functools.partial(solve_kernel, pair, by_shift),
        out_shape=shape,
        grid=(1,),
        in_specs=[
            pl.BlockSpec((2, 2 * M, M), lambda i: (pair, 0, 0)),
            pl.BlockSpec((2 * M, M), lambda i: (0, 0)),
            pl.BlockSpec((M, M), lambda i: (0, 0)),
            smem(),
            smem(),
        ],
        out_specs=specs,
        scratch_shapes=[
            pltpu.VMEM((2, M, M), F32),
            pltpu.VMEM((2, M, M), F32),
            pltpu.VMEM((2, 2 * M, M), F32),
        ],
        compiler_params=pltpu.CompilerParams(vmem_limit_bytes=LIMIT),
        cost_estimate=pl.CostEstimate(flops=3_400_000_000, bytes_accessed=3_000_000, transcendentals=0),
        name="solve_points",
    )(sigma, ham, coupling, energies, counts)


def lorentz(offset):
    scaled = offset / BROADENING
    return 1.0 / (1.0 + scaled * scaled)


def operator_kernel(row_ref, col_ref, strength_ref, offset_ref, high_ref, low_ref, weight_ref):
    rows = 512
    spacing = row_ref[...][:, :1] - col_ref[...][:1, :]
    values = lorentz(spacing - PHONON) + lorentz(spacing + PHONON)
    row_id = lax.broadcasted_iota(jnp.int32, (rows, rows), 0)
    col_id = lax.broadcasted_iota(jnp.int32, (rows, rows), 1)
    values = jnp.where(((row_id ^ col_id) & 3) == 0, values, 0.0)
    values = values / jnp.sum(values, axis=1, keepdims=True)
    high, low = split(values)
    high_ref[...] = high
    low_ref[...] = low
    for d in range(KN):
        total = jnp.float32(0.0)
        for j in range(16):
            total = total + jnp.where(offset_ref[j] == d, strength_ref[j], 0.0)
        weight_ref[d] = total


def build_operator(row_energy, col_energy, strengths, offsets):
    return pl.pallas_call(
        operator_kernel,
        out_shape=[
            jax.ShapeDtypeStruct((512, 512), BF16),
            jax.ShapeDtypeStruct((512, 512), BF16),
            jax.ShapeDtypeStruct((KN,), F32),
        ],
        in_specs=[vmem(), vmem(), smem(), smem()],
        out_specs=[vmem(), vmem(), smem()],
        compiler_params=pltpu.CompilerParams(vmem_limit_bytes=LIMIT),
        cost_estimate=pl.CostEstimate(flops=10_000_000, bytes_accessed=1_500_000, transcendentals=0),
        name="energy_operator",
    )(row_energy, col_energy, strengths, offsets)


def mix_kernel(high_ref, low_ref, weight_ref, a_ref, *rest):
    b_refs, out_a, out_b, (x_high, x_low, y_ref) = rest[:8], rest[8:16], rest[16], rest[17:]
    weight = [weight_ref[d] for d in range(KN)]
    for e in range(E4):
        for d in range(ZN):
            for chunk in range(2):
                row = chunk * 256 + (e * ZN + d) * 8
                if chunk == 0:
                    given = [a_ref[e * KN + k, d] for k in range(KN)]
                else:
                    given = [b_refs[d][e * KN + k] for k in range(KN)]
                for k in range(KN):
                    total = weight[0] * given[k]
                    for s in range(1, KN):
                        total = total + weight[s] * given[(k - s) % KN]
                    y_ref[pl.ds(row, 8), k * 128 : k * 128 + 128] = total
    mixed = y_ref[...]
    high, low = split(mixed)
    x_high[...] = high
    x_low[...] = low
    left = jnp.concatenate([high_ref[...], high_ref[...], low_ref[...]], axis=1)
    for half in range(2):
        lanes = pl.ds(half * 512, 512)
        right = jnp.concatenate([x_high[:, lanes], x_low[:, lanes], x_high[:, lanes]], axis=0)
        y_ref[:, lanes] = jnp.dot(left, right, preferred_element_type=F32)
    for e in range(E4):
        for d in range(ZN):
            for k in range(KN):
                row = (e * ZN + d) * 8
                lanes = pl.ds(k * 128, 128)
                out_a[d][e * KN + k] = y_ref[pl.ds(row, 8), lanes]
                out_b[e * KN + k, d] = y_ref[pl.ds(256 + row, 8), lanes]


def mix(operator, a, b):
    high, low, weights = operator
    return pl.pallas_call(
        mix_kernel,
        out_shape=[jax.ShapeDtypeStruct((WN, 8, 128), F32)] * ZN
        + [jax.ShapeDtypeStruct((WN, ZN, 8, 128), F32)],
        in_specs=[vmem(), vmem(), smem(), vmem()] + [vmem()] * ZN,
        out_specs=[vmem()] * (ZN + 1),
        scratch_shapes=[
            pltpu.VMEM((512, 1024), BF16),
            pltpu.VMEM((512, 1024), BF16),
            pltpu.VMEM((512, 1024), F32),
        ],
        compiler_params=pltpu.CompilerParams(vmem_limit_bytes=LIMIT),
        cost_estimate=pl.CostEstimate(flops=1_600_000_000, bytes_accessed=5_000_000, transcendentals=0),
        name="mix_energies",
    )(high, low, weights, a, *b)


def blend_kernel(sigma_ref, a_ref, *rest):
    b_refs, out_ref = rest[:8], rest[8]
    z = lax.axis_index("z")
    for d in range(ZN):
        slab = lax.rem(z - d + ZN, ZN) * SLAB
        for t in range(SLAB // 8):
            rows = pl.ds(pl.multiple_of(slab + 8 * t, 8), 8)
            for half in range(2):
                lanes = slice(half * 128, half * 128 + 128)
                w = 4 * t + half
                low = swap_halves(a_ref[w, d], a_ref[w + 2, d])
                high = swap_halves(b_refs[d][w], b_refs[d][w + 2])
                for p, tile in enumerate(low + high):
                    old = sigma_ref[p, rows, lanes]
                    out_ref[p, rows, lanes] = (1.0 - MIX_RATE) * old + MIX_RATE * tile


def blend(sigma, a, b):
    return pl.pallas_call(
        blend_kernel,
        out_shape=jax.ShapeDtypeStruct((PTS, 2 * M, M), F32),
        in_specs=[vmem()] * (2 + ZN),
        out_specs=vmem(),
        compiler_params=pltpu.CompilerParams(vmem_limit_bytes=LIMIT),
        cost_estimate=pl.CostEstimate(flops=2_000_000, bytes_accessed=6_000_000, transcendentals=0),
        name="blend_old",
    )(sigma, a, *b)


def along_z(pieces):
    moved = [pieces[0]]
    for d in range(1, ZN):
        moved.append(lax.ppermute(pieces[d], "z", [(i, (i + d) % ZN) for i in range(ZN)]))
    return moved


def in_plane(x):
    return lax.all_to_all(x, PLANE, split_axis=0, concat_axis=0, tiled=True)


def energy_rows(energies, z):
    grid = energies.reshape(2, ZN, 2, 2, 2)
    twice = jnp.concatenate([grid, grid], axis=1)
    ahead = lax.dynamic_slice_in_dim(twice, z, ZN, 1)
    turned = jnp.flip(twice, axis=1)
    behind = lax.dynamic_slice_in_dim(turned, ZN - 1 - z, ZN, 1)

    def order(part):
        moved = jnp.transpose(part, (3, 0, 2, 1, 4)).reshape(-1)
        return jnp.repeat(moved, 4)

    return order(ahead), order(behind)


def body(sigma_in, hamiltonian, coupling, energies, counts, strengths, offsets):
    sigma = sigma_in.reshape(PTS, 2 * M, M)
    ham = hamiltonian.reshape(2 * M, M)
    coup = coupling.reshape(M, M)
    z = lax.axis_index("z")

    a = solve(0, True, sigma, ham, coup, energies, counts)
    a = along_z(a)
    (b,) = solve(1, False, sigma, ham, coup, energies, counts)
    rows, cols = energy_rows(energies, z)
    operator = build_operator(
        jnp.broadcast_to(rows[:, None], (512, 128)),
        jnp.broadcast_to(cols[None, :], (8, 512)),
        strengths,
        offsets,
    )
    b = in_plane(b)
    b = along_z([b[:, d] for d in range(ZN)])
    a = in_plane(jnp.stack(a, axis=1))
    out = mix(operator, a, b)
    a, b = out[:ZN], out[ZN]
    a = along_z(a)
    b = in_plane(b)
    b = along_z([b[:, d] for d in range(ZN)])
    a = in_plane(jnp.stack(a, axis=1))
    return blend(sigma, a, b).reshape(sigma_in.shape)


def solution(mesh):
    fine = Mesh(mesh.devices.reshape(2, ZN, 2, 2, 4), ("xl", "z", "c", "xh", "y"))
    energy, mom = ("xl", "z", "c"), ("xh", "y")
    return jax.shard_map(
        body,
        mesh=fine,
        in_specs=(
            P(energy, mom, None, None, None),
            P(mom, None, None, None),
            P(mom, None, None),
            P(),
            P(),
            P(),
            P(),
        ),
        out_specs=P(energy, mom, None, None, None),
        check_vma=False,
    )
```

```python
import jax
import jax.numpy as jnp
from jax import lax
from jax.experimental import pallas as pl
from jax.experimental.pallas import tpu as pltpu
from jax.sharding import Mesh
from jax.sharding import PartitionSpec as P

MIX_RATE = 0.6
PHONON = 0.1
BROADENING = 0.02

M = 256
PTS = 4
E_TOT = 128
KN = 8
DEVS = 256
ROWS = 16
ORDER = ("xl", "xh", "y", "z", "c")
F32 = jnp.float32
BF16 = jnp.bfloat16
LIMIT = 58 * 1024 * 1024


def vmem():
    return pl.BlockSpec(memory_space=pltpu.VMEM)


def smem():
    return pl.BlockSpec(memory_space=pltpu.SMEM)


def split(x):
    high = x.astype(BF16)
    return high, (x - high.astype(F32)).astype(BF16)


def dot3(a, b):
    left = jnp.concatenate([a[0], a[0], a[1]], axis=1)
    right = jnp.concatenate([b[0], b[1], b[0]], axis=0)
    return jnp.dot(left, right, preferred_element_type=F32)


def both(top, bottom):
    return tuple(jnp.concatenate([t, b], axis=0) for t, b in zip(top, bottom))


def swap_halves(x, y):
    low = lax.broadcasted_iota(jnp.int32, x.shape, x.ndim - 2) < 4
    axis = x.ndim - 2
    first = jnp.where(low, x, pltpu.roll(y, 4, axis))
    second = jnp.where(low, pltpu.roll(x, 4, axis), y)
    return first, second


def invert_all(residuals, scales, slow):
    rows = lax.broadcasted_iota(jnp.int32, (M, M), 0)
    cols = lax.broadcasted_iota(jnp.int32, (M, M), 1)
    eye = (rows == cols).astype(F32)
    pairs = [split(r) for r in residuals]
    squares = [split(dot3(p, p)) for p in pairs]
    firsts = [(eye + r) * s for r, s in zip(residuals, scales)]
    stacked = [dot3(both(split(f), q), q) for f, q in zip(firsts, squares)]
    seconds = [f + s[:M] for f, s in zip(firsts, stacked)]
    fourths = [split(s[M:]) for s in stacked]
    stacked = [dot3(both(split(x), q), q) for x, q in zip(seconds, fourths)]
    thirds = [x + s[:M] for x, s in zip(seconds, stacked)]
    lasts = [x + dot3(split(x), split(s[M:])) for x, s in zip(thirds, stacked)]
    return [jnp.where(f, last, second) for f, last, second in zip(slow, lasts, seconds)]


def solve_kernel(sigma_ref, ham_ref, coup_ref, energy_ref, count_ref, out_ref, green_ref):
    rank = (lax.axis_index("xl") * 8 + lax.axis_index("z")) * 2 + lax.axis_index("c")
    coupling = split(coup_ref[...])
    turned = split(coup_ref[...].T)
    for group in range(2):
        points = (2 * group, 2 * group + 1)
        energy = [energy_ref[rank * PTS + p] for p in points]
        slow = [count_ref[rank * PTS + p] > 2 for p in points]
        scale = [1.0 / jnp.full((M, M), e, F32) for e in energy]
        residual = [(ham_ref[:M] + sigma_ref[p, :M]) * s for p, s in zip(points, scale)]
        left = invert_all(residual, scale, slow)
        inverse = [split(x) for x in left]
        coupled = [split(dot3(x, coupling)) for x in inverse]
        back = [split(dot3(turned, x)) for x in inverse]
        residual = [
            (ham_ref[M:] + sigma_ref[p, M:] + dot3(turned, c)) * s
            for p, c, s in zip(points, coupled, scale)
        ]
        right = invert_all(residual, scale, slow)
        through = [split(dot3(c, split(r))) for c, r in zip(coupled, right)]
        for i in range(2):
            green_ref[i, :M] = left[i] + dot3(through[i], back[i])
            green_ref[i, M:] = right[i]
        for block in range(8):
            slab = slice(block * 64, block * 64 + 64)
            first = green_ref[0, slab].reshape(8, 8, M)
            second = green_ref[1, slab].reshape(8, 8, M)
            for parity, tiles in enumerate(swap_halves(first, second)):
                for t in range(8):
                    for half in range(2):
                        piece = block * 32 + 4 * t + 2 * parity + half
                        lanes = slice(half * 128, half * 128 + 128)
                        out_ref[piece, group * 8 : group * 8 + 8] = tiles[t, :, lanes]


def solve(sigma, ham, coupling, energies, counts):
    return pl.pallas_call(
        solve_kernel,
        out_shape=jax.ShapeDtypeStruct((DEVS, ROWS, 128), F32),
        in_specs=[vmem(), vmem(), vmem(), smem(), smem()],
        out_specs=vmem(),
        scratch_shapes=[pltpu.VMEM((2, 2 * M, M), F32)],
        compiler_params=pltpu.CompilerParams(vmem_limit_bytes=LIMIT),
        cost_estimate=pl.CostEstimate(flops=6_800_000_000, bytes_accessed=5_000_000, transcendentals=0),
        name="solve_points",
    )(sigma, ham, coupling, energies, counts)


def lorentz(offset):
    scaled = offset / BROADENING
    return 1.0 / (1.0 + scaled * scaled)


def operator_kernel(energy_ref, strength_ref, offset_ref, high_ref, low_ref, weight_ref):
    columns = jnp.broadcast_to(energy_ref[...], (E_TOT, E_TOT))
    spacing = columns.T - columns
    values = lorentz(spacing - PHONON) + lorentz(spacing + PHONON)
    values = values / jnp.sum(values, axis=1, keepdims=True)
    wide = E_TOT * 4
    spread = (
        lax.broadcasted_iota(jnp.int32, (wide, E_TOT), 0) // 4
        == lax.broadcasted_iota(jnp.int32, (wide, E_TOT), 1)
    ).astype(BF16)
    gather = (
        lax.broadcasted_iota(jnp.int32, (E_TOT, wide), 1) // 4
        == lax.broadcasted_iota(jnp.int32, (E_TOT, wide), 0)
    ).astype(BF16)
    row_id = lax.broadcasted_iota(jnp.int32, (wide, wide), 0)
    col_id = lax.broadcasted_iota(jnp.int32, (wide, wide), 1)
    same = ((row_id ^ col_id) & 3) == 0
    for part, ref in zip(split(values), (high_ref, low_ref)):
        tall = jnp.dot(spread, part, preferred_element_type=F32).astype(BF16)
        full = jnp.dot(tall, gather, preferred_element_type=F32)
        ref[...] = jnp.where(same, full, 0.0).astype(BF16)
    for d in range(KN):
        total = jnp.float32(0.0)
        for j in range(16):
            total = total + jnp.where(offset_ref[j] == d, strength_ref[j], 0.0)
        weight_ref[d] = total


def build_operator(energies, strengths, offsets):
    return pl.pallas_call(
        operator_kernel,
        out_shape=[
            jax.ShapeDtypeStruct((512, 512), BF16),
            jax.ShapeDtypeStruct((512, 512), BF16),
            jax.ShapeDtypeStruct((KN,), F32),
        ],
        in_specs=[vmem(), smem(), smem()],
        out_specs=[vmem(), vmem(), smem()],
        compiler_params=pltpu.CompilerParams(vmem_limit_bytes=16 * 1024 * 1024),
        cost_estimate=pl.CostEstimate(flops=150_000_000, bytes_accessed=1_500_000, transcendentals=0),
        name="energy_operator",
    )(energies, strengths, offsets)


def mix_kernel(high_ref, low_ref, weight_ref, in_ref, out_ref, x_high, x_low):
    weight = [weight_ref[d] for d in range(KN)]
    for upper in range(2):
        for device in range(16):
            given = [in_ref[(upper * KN + k) * 16 + device] for k in range(KN)]
            row = (upper * 16 + device) * ROWS
            for k in range(KN):
                total = weight[0] * given[k]
                for s in range(1, KN):
                    total = total + weight[s] * given[(k - s) % KN]
                high, low = split(total)
                x_high[row : row + ROWS, k * 128 : k * 128 + 128] = high
                x_low[row : row + ROWS, k * 128 : k * 128 + 128] = low
    left = jnp.concatenate([high_ref[...], high_ref[...], low_ref[...]], axis=1)
    for pair in range(KN // 2):
        lanes = slice(pair * 256, pair * 256 + 256)
        right = jnp.concatenate([x_high[:, lanes], x_low[:, lanes], x_high[:, lanes]], axis=0)
        mixed = jnp.dot(left, right, preferred_element_type=F32)
        for k in (2 * pair, 2 * pair + 1):
            part = mixed[:, (k % 2) * 128 : (k % 2) * 128 + 128].reshape(32, ROWS, 128)
            for upper in range(2):
                first = (upper * KN + k) * 16
                out_ref[first : first + 16] = part[upper * 16 : upper * 16 + 16]


def mix(operator, x):
    return pl.pallas_call(
        mix_kernel,
        out_shape=jax.ShapeDtypeStruct((DEVS, ROWS, 128), F32),
        in_specs=[vmem(), vmem(), smem(), vmem()],
        out_specs=vmem(),
        scratch_shapes=[pltpu.VMEM((512, 1024), BF16), pltpu.VMEM((512, 1024), BF16)],
        compiler_params=pltpu.CompilerParams(vmem_limit_bytes=24 * 1024 * 1024),
        cost_estimate=pl.CostEstimate(flops=1_600_000_000, bytes_accessed=5_000_000, transcendentals=0),
        name="mix_energies",
    )(*operator, x)


def blend_kernel(sigma_ref, in_ref, out_ref):
    for t in range(16):
        rows = slice(8 * t, 8 * t + 8)
        for half in range(2):
            lanes = slice(half * 128, half * 128 + 128)
            even = in_ref[4 * t + half]
            odd = in_ref[4 * t + 2 + half]
            tiles = swap_halves(even[:8], odd[:8]) + swap_halves(even[8:], odd[8:])
            for p, tile in enumerate(tiles):
                old = sigma_ref[p, rows, lanes]
                out_ref[p, rows, lanes] = (1.0 - MIX_RATE) * old + MIX_RATE * tile


def blend(sigma, x):
    steps = 4
    rows = 2 * M // steps
    return pl.pallas_call(
        blend_kernel,
        out_shape=jax.ShapeDtypeStruct((PTS, 2 * M, M), F32),
        grid=(steps,),
        in_specs=[
            pl.BlockSpec((PTS, rows, M), lambda i: (0, i, 0)),
            pl.BlockSpec((DEVS // steps, ROWS, 128), lambda i: (i, 0, 0)),
        ],
        out_specs=pl.BlockSpec((PTS, rows, M), lambda i: (0, i, 0)),
        compiler_params=pltpu.CompilerParams(vmem_limit_bytes=16 * 1024 * 1024),
        cost_estimate=pl.CostEstimate(flops=2_000_000, bytes_accessed=6_000_000, transcendentals=0),
        name="blend_old",
    )(sigma, x)


def exchange(x):
    return lax.all_to_all(x, ORDER, split_axis=0, concat_axis=0, tiled=True)


def body(sigma_in, hamiltonian, coupling, energies, counts, strengths, offsets):
    sigma = sigma_in.reshape(PTS, 2 * M, M)
    green = solve(sigma, hamiltonian.reshape(2 * M, M), coupling.reshape(M, M), energies, counts)
    columns = exchange(green)
    operator = build_operator(energies.reshape(1, E_TOT), strengths, offsets)
    result = exchange(mix(operator, columns))
    return blend(sigma, result).reshape(sigma_in.shape)


def solution(mesh):
    fine = Mesh(mesh.devices.reshape(2, 8, 2, 2, 4), ("xl", "z", "c", "xh", "y"))
    energy, mom = ("xl", "z", "c"), ("xh", "y")
    return jax.shard_map(
        body,
        mesh=fine,
        in_specs=(
            P(energy, mom, None, None, None),
            P(mom, None, None, None),
            P(mom, None, None),
            P(),
            P(),
            P(),
            P(),
        ),
        out_specs=P(energy, mom, None, None, None),
        check_vma=False,
    )
```

```python
import jax
import jax.numpy as jnp
from jax import lax
from jax.experimental import pallas as pl
from jax.experimental.pallas import tpu as pltpu
from jax.sharding import Mesh
from jax.sharding import PartitionSpec as P

MIX_RATE = 0.6
PHONON = 0.1
BROADENING = 0.02

M = 256
PTS = 4
E_TOT = 128
KN = 8
DEVS = 256
ROWS = 16
ORDER = ("xl", "xh", "y", "z", "c")
F32 = jnp.float32
BF16 = jnp.bfloat16


def vmem():
    return pl.BlockSpec(memory_space=pltpu.VMEM)


def smem():
    return pl.BlockSpec(memory_space=pltpu.SMEM)


def split(x):
    high = x.astype(BF16)
    return high, (x - high.astype(F32)).astype(BF16)


def dot3(a, b):
    left = jnp.concatenate([a[0], a[0], a[1]], axis=1)
    right = jnp.concatenate([b[0], b[1], b[0]], axis=0)
    return jnp.dot(left, right, preferred_element_type=F32)


def both(top, bottom):
    return tuple(jnp.concatenate([t, b], axis=0) for t, b in zip(top, bottom))


def swap_halves(x, y):
    low = lax.broadcasted_iota(jnp.int32, x.shape, x.ndim - 2) < 4
    axis = x.ndim - 2
    first = jnp.where(low, x, pltpu.roll(y, 4, axis))
    second = jnp.where(low, pltpu.roll(x, 4, axis), y)
    return first, second


def invert_all(residuals, scales, slow):
    rows = lax.broadcasted_iota(jnp.int32, (M, M), 0)
    cols = lax.broadcasted_iota(jnp.int32, (M, M), 1)
    eye = (rows == cols).astype(F32)
    pairs = [split(r) for r in residuals]
    squares = [split(dot3(p, p)) for p in pairs]
    firsts = [(eye + r) * s for r, s in zip(residuals, scales)]
    stacked = [dot3(both(split(f), q), q) for f, q in zip(firsts, squares)]
    seconds = [f + s[:M] for f, s in zip(firsts, stacked)]
    fourths = [split(s[M:]) for s in stacked]
    stacked = [dot3(both(split(x), q), q) for x, q in zip(seconds, fourths)]
    thirds = [x + s[:M] for x, s in zip(seconds, stacked)]
    lasts = [x + dot3(split(x), split(s[M:])) for x, s in zip(thirds, stacked)]
    return [jnp.where(f, last, second) for f, last, second in zip(slow, lasts, seconds)]


def to_pieces(green, out_ref, base):
    for block in range(4):
        slab = slice(block * 64, block * 64 + 64)
        for group in range(2):
            first = green[2 * group][slab].reshape(8, 8, M)
            second = green[2 * group + 1][slab].reshape(8, 8, M)
            for parity, tiles in enumerate(swap_halves(first, second)):
                for t in range(8):
                    for half in range(2):
                        piece = base + block * 32 + 4 * t + 2 * parity + half
                        lanes = slice(half * 128, half * 128 + 128)
                        out_ref[piece, group * 8 : group * 8 + 8] = tiles[t, :, lanes]


def solve_kernel(
    sigma_hbm,
    ham_hbm,
    coup_hbm,
    energy_ref,
    count_ref,
    out_hbm,
    out_ref,
    sigma_ref,
    ham_ref,
    coup_ref,
    sems,
):
    upper, lower = pl.ds(0, M), pl.ds(M, M)
    copies = [
        pltpu.make_async_copy(ham_hbm.at[upper], ham_ref.at[upper], sems.at[0]),
        *(
            pltpu.make_async_copy(sigma_hbm.at[p, upper], sigma_ref.at[p, upper], sems.at[1 + p])
            for p in range(PTS)
        ),
        pltpu.make_async_copy(coup_hbm, coup_ref, sems.at[5]),
        pltpu.make_async_copy(ham_hbm.at[lower], ham_ref.at[lower], sems.at[6]),
        pltpu.make_async_copy(sigma_hbm.at[:, lower], sigma_ref.at[:, lower], sems.at[7]),
    ]
    for copy in copies:
        copy.start()
    rank = (lax.axis_index("xl") * 8 + lax.axis_index("z")) * 2 + lax.axis_index("c")
    points = range(PTS)
    energy = [energy_ref[rank * PTS + p] for p in points]
    slow = [count_ref[rank * PTS + p] > 2 for p in points]
    scale = [1.0 / jnp.full((M, M), e, F32) for e in energy]
    copies[0].wait()
    residual = []
    for p in points:
        copies[1 + p].wait()
        residual.append((ham_ref[:M] + sigma_ref[p, :M]) * scale[p])
    left = invert_all(residual, scale, slow)
    for copy in copies[5:]:
        copy.wait()
    coupling = split(coup_ref[...])
    turned = split(coup_ref[...].T)
    inverse = [split(x) for x in left]
    coupled = [split(dot3(x, coupling)) for x in inverse]
    back = [split(dot3(turned, x)) for x in inverse]
    residual = [
        (ham_ref[M:] + sigma_ref[p, M:] + dot3(turned, coupled[p])) * scale[p] for p in points
    ]
    right = invert_all(residual, scale, slow)
    to_pieces(right, out_ref, 128)
    half = pl.ds(128, 128)
    sent = pltpu.make_async_copy(out_ref.at[half], out_hbm.at[half], sems.at[8])
    sent.start()
    through = [split(dot3(c, split(r))) for c, r in zip(coupled, right)]
    to_pieces([x + dot3(t, b) for x, t, b in zip(left, through, back)], out_ref, 0)
    half = pl.ds(0, 128)
    last = pltpu.make_async_copy(out_ref.at[half], out_hbm.at[half], sems.at[9])
    last.start()
    sent.wait()
    last.wait()


def solve(sigma, ham, coupling, energies, counts):
    hbm = pl.BlockSpec(memory_space=pltpu.HBM)
    return pl.pallas_call(
        solve_kernel,
        out_shape=jax.ShapeDtypeStruct((DEVS, ROWS, 128), F32),
        in_specs=[hbm, hbm, hbm, smem(), smem()],
        out_specs=hbm,
        scratch_shapes=[
            pltpu.VMEM((DEVS, ROWS, 128), F32),
            pltpu.VMEM((PTS, 2 * M, M), F32),
            pltpu.VMEM((2 * M, M), F32),
            pltpu.VMEM((M, M), F32),
            pltpu.SemaphoreType.DMA((10,)),
        ],
        compiler_params=pltpu.CompilerParams(vmem_limit_bytes=60 * 1024 * 1024),
        cost_estimate=pl.CostEstimate(flops=6_800_000_000, bytes_accessed=5_000_000, transcendentals=0),
        name="solve_points",
    )(sigma, ham, coupling, energies, counts)


def lorentz(offset):
    scaled = offset / BROADENING
    return 1.0 / (1.0 + scaled * scaled)


def energy_operator(energies):
    columns = jnp.broadcast_to(energies, (E_TOT, E_TOT))
    spacing = columns.T - columns
    values = lorentz(spacing - PHONON) + lorentz(spacing + PHONON)
    values = values / jnp.sum(values, axis=1, keepdims=True)
    wide = E_TOT * 4
    spread = (
        lax.broadcasted_iota(jnp.int32, (wide, E_TOT), 0) // 4
        == lax.broadcasted_iota(jnp.int32, (wide, E_TOT), 1)
    ).astype(BF16)
    gather = (
        lax.broadcasted_iota(jnp.int32, (E_TOT, wide), 1) // 4
        == lax.broadcasted_iota(jnp.int32, (E_TOT, wide), 0)
    ).astype(BF16)
    row_id = lax.broadcasted_iota(jnp.int32, (wide, wide), 0)
    col_id = lax.broadcasted_iota(jnp.int32, (wide, wide), 1)
    same = ((row_id ^ col_id) & 3) == 0
    parts = []
    for part in split(values):
        tall = jnp.dot(spread, part, preferred_element_type=F32).astype(BF16)
        full = jnp.dot(tall, gather, preferred_element_type=F32)
        parts.append(jnp.where(same, full, 0.0).astype(BF16))
    return parts


def mix_kernel(energy_ref, strength_ref, offset_ref, in_ref, out_ref, high_ref, low_ref, x_high, x_low):
    weight = []
    for d in range(KN):
        total = jnp.float32(0.0)
        for j in range(16):
            total = total + jnp.where(offset_ref[j] == d, strength_ref[j], 0.0)
        weight.append(total)
    high_ref[...], low_ref[...] = energy_operator(energy_ref[...])
    for pair in range(KN // 2):
        targets = (2 * pair, 2 * pair + 1)
        for upper in range(2):
            for device in range(16):
                given = [in_ref[(upper * KN + k) * 16 + device] for k in range(KN)]
                row = (upper * 16 + device) * ROWS
                for k in targets:
                    total = weight[0] * given[k]
                    for s in range(1, KN):
                        total = total + weight[s] * given[(k - s) % KN]
                    high, low = split(total)
                    x_high[row : row + ROWS, k * 128 : k * 128 + 128] = high
                    x_low[row : row + ROWS, k * 128 : k * 128 + 128] = low
        lanes = slice(pair * 256, pair * 256 + 256)
        high, low = high_ref[...], low_ref[...]
        left = jnp.concatenate([high, high, low], axis=1)
        right = jnp.concatenate([x_high[:, lanes], x_low[:, lanes], x_high[:, lanes]], axis=0)
        mixed = jnp.dot(left, right, preferred_element_type=F32)
        for k in targets:
            part = mixed[:, (k % 2) * 128 : (k % 2) * 128 + 128].reshape(32, ROWS, 128)
            for upper in range(2):
                first = (upper * KN + k) * 16
                out_ref[first : first + 16] = part[upper * 16 : upper * 16 + 16]


def mix(energies, strengths, offsets, x):
    return pl.pallas_call(
        mix_kernel,
        out_shape=jax.ShapeDtypeStruct((DEVS, ROWS, 128), F32),
        in_specs=[vmem(), smem(), smem(), vmem()],
        out_specs=vmem(),
        scratch_shapes=[
            pltpu.VMEM((512, 512), BF16),
            pltpu.VMEM((512, 512), BF16),
            pltpu.VMEM((512, 1024), BF16),
            pltpu.VMEM((512, 1024), BF16),
        ],
        compiler_params=pltpu.CompilerParams(vmem_limit_bytes=32 * 1024 * 1024),
        cost_estimate=pl.CostEstimate(flops=1_700_000_000, bytes_accessed=4_200_000, transcendentals=0),
        name="mix_energies",
    )(energies, strengths, offsets, x)


def blend_kernel(sigma_ref, in_ref, out_hbm, out_ref, sems):
    copies = []
    for block in range(4):
        for t in range(16 * block, 16 * block + 16):
            rows = slice(8 * t, 8 * t + 8)
            for half in range(2):
                lanes = slice(half * 128, half * 128 + 128)
                even = in_ref[4 * t + half]
                odd = in_ref[4 * t + 2 + half]
                tiles = swap_halves(even[:8], odd[:8]) + swap_halves(even[8:], odd[8:])
                for p, tile in enumerate(tiles):
                    old = sigma_ref[p, rows, lanes]
                    out_ref[p, rows, lanes] = (1.0 - MIX_RATE) * old + MIX_RATE * tile
        rows = pl.ds(128 * block, 128)
        copies.append(
            pltpu.make_async_copy(out_ref.at[:, rows], out_hbm.at[:, rows], sems.at[block])
        )
        copies[-1].start()
    for copy in copies:
        copy.wait()


def blend(sigma, x):
    return pl.pallas_call(
        blend_kernel,
        out_shape=jax.ShapeDtypeStruct((PTS, 2 * M, M), F32),
        in_specs=[vmem(), vmem()],
        out_specs=pl.BlockSpec(memory_space=pltpu.HBM),
        scratch_shapes=[pltpu.VMEM((PTS, 2 * M, M), F32), pltpu.SemaphoreType.DMA((4,))],
        compiler_params=pltpu.CompilerParams(vmem_limit_bytes=24 * 1024 * 1024),
        cost_estimate=pl.CostEstimate(flops=2_000_000, bytes_accessed=6_000_000, transcendentals=0),
        name="blend_old",
    )(sigma, x)


def exchange(x):
    return lax.all_to_all(x, ORDER, split_axis=0, concat_axis=0, tiled=True)


def body(sigma_in, hamiltonian, coupling, energies, counts, strengths, offsets):
    sigma = sigma_in.reshape(PTS, 2 * M, M)
    green = solve(sigma, hamiltonian.reshape(2 * M, M), coupling.reshape(M, M), energies, counts)
    columns = exchange(green)
    mixed = mix(energies.reshape(1, E_TOT), strengths, offsets, columns)
    result = exchange(mixed)
    return blend(sigma, result).reshape(sigma_in.shape)


def solution(mesh):
    fine = Mesh(mesh.devices.reshape(2, 8, 2, 2, 4), ("xl", "z", "c", "xh", "y"))
    energy, mom = ("xl", "z", "c"), ("xh", "y")
    return jax.shard_map(
        body,
        mesh=fine,
        in_specs=(
            P(energy, mom, None, None, None),
            P(mom, None, None, None),
            P(mom, None, None),
            P(),
            P(),
            P(),
            P(),
        ),
        out_specs=P(energy, mom, None, None, None),
        check_vma=False,
    )
```

```python
import jax
import jax.numpy as jnp
from jax import lax
from jax.experimental import pallas as pl
from jax.experimental.pallas import tpu as pltpu
from jax.sharding import Mesh
from jax.sharding import PartitionSpec as P

MIX_RATE = 0.6
PHONON = 0.1
BROADENING = 0.02
GOLDEN = 0.5 + 0.5 * 5.0**0.5

M = 256
PTS = 4
E_TOT = 128
KN = 8
DEVS = 256
ROWS = 16
ORDER = ("xl", "xh", "y", "z", "c")
F32 = jnp.float32
BF16 = jnp.bfloat16


def vmem():
    return pl.BlockSpec(memory_space=pltpu.VMEM)


def smem():
    return pl.BlockSpec(memory_space=pltpu.SMEM)


def split(x):
    high = x.astype(BF16)
    return high, (x - high.astype(F32)).astype(BF16)


def dot3(a, b):
    left = jnp.concatenate([a[0], a[0], a[1]], axis=1)
    right = jnp.concatenate([b[0], b[1], b[0]], axis=0)
    return jnp.dot(left, right, preferred_element_type=F32)


def exchange_rows(x, y, group):
    axis = x.ndim - 2
    even = lax.broadcasted_iota(jnp.int32, x.shape, axis) // group % 2 == 0
    first = jnp.where(even, x, pltpu.roll(y, group, axis))
    second = jnp.where(even, pltpu.roll(x, 8 - group, axis), y)
    return first, second


def transpose_rows(tiles):
    a, c = exchange_rows(tiles[0], tiles[2], 4)
    b, d = exchange_rows(tiles[1], tiles[3], 4)
    return exchange_rows(a, b, 2) + exchange_rows(c, d, 2)


def invert_all(residuals, scales, slow):
    rows = lax.broadcasted_iota(jnp.int32, (M, M), 0)
    cols = lax.broadcasted_iota(jnp.int32, (M, M), 1)
    eye = (rows == cols).astype(F32)
    pairs = [split(r) for r in residuals]
    seconds = [dot3(p, p) for p in pairs]
    thirds = [dot3(split(q), p) for q, p in zip(seconds, pairs)]
    sums = [r + q + t for r, q, t in zip(residuals, seconds, thirds)]
    cubes = [split(t) for t in thirds]
    sixths = [dot3(c, c) + eye for c in cubes]
    quartics = [
        dot3(split(u + GOLDEN * t), split(u - (1.0 / GOLDEN) * t)) for u, t in zip(sixths, thirds)
    ]
    longs = [dot3(split(r), split(q)) for r, q in zip(sums, quartics)]
    return [
        (eye + jnp.where(f, x, r)) * s for f, x, r, s in zip(slow, longs, sums, scales)
    ]


def to_pieces(green, out_ref, base, block):
    slab = slice(block * 64, block * 64 + 64)
    for q, tiles in enumerate(transpose_rows([g[slab].reshape(8, 8, M) for g in green])):
        for t in range(8):
            for half in range(2):
                piece = base + block * 32 + 4 * t + 2 * (q // 2) + half
                rows = slice(q % 2 * 8, q % 2 * 8 + 8)
                out_ref[piece, rows] = tiles[t, :, half * 128 : half * 128 + 128]


def solve_kernel(
    sigma_hbm,
    ham_hbm,
    coup_hbm,
    energy_ref,
    count_ref,
    out_hbm,
    out_ref,
    sigma_ref,
    ham_ref,
    coup_ref,
    sems,
):
    upper, lower = pl.ds(0, M), pl.ds(M, M)
    copies = [
        pltpu.make_async_copy(coup_hbm, coup_ref, sems.at[0]),
        pltpu.make_async_copy(ham_hbm.at[upper], ham_ref.at[upper], sems.at[1]),
        *(
            pltpu.make_async_copy(sigma_hbm.at[p, upper], sigma_ref.at[p, upper], sems.at[2 + p])
            for p in range(PTS)
        ),
        pltpu.make_async_copy(ham_hbm.at[lower], ham_ref.at[lower], sems.at[6]),
        pltpu.make_async_copy(sigma_hbm.at[:, lower], sigma_ref.at[:, lower], sems.at[7]),
    ]
    for copy in copies:
        copy.start()
    rank = (lax.axis_index("xl") * 8 + lax.axis_index("z")) * 2 + lax.axis_index("c")
    points = range(PTS)
    energy = [energy_ref[rank * PTS + p] for p in points]
    slow = [count_ref[rank * PTS + p] > 2 for p in points]
    scale = [1.0 / jnp.full((M, M), e, F32) for e in energy]
    copies[0].wait()
    coupling = split(coup_ref[...])
    turned = split(coup_ref[...].T)
    copies[1].wait()
    residual = []
    for p in points:
        copies[2 + p].wait()
        residual.append((ham_ref[:M] + sigma_ref[p, :M]) * scale[p])
    left = invert_all(residual, scale, slow)
    for copy in copies[6:]:
        copy.wait()
    inverse = [split(x) for x in left]
    coupled = [split(dot3(x, coupling)) for x in inverse]
    back = [split(dot3(turned, x)) for x in inverse]
    residual = [
        (ham_ref[M:] + sigma_ref[p, M:] + dot3(turned, coupled[p])) * scale[p] for p in points
    ]
    right = invert_all(residual, scale, slow)
    through = [split(dot3(c, split(r))) for c, r in zip(coupled, right)]
    sent = []
    for base, green in ((128, right), (0, None)):
        if green is None:
            green = [x + dot3(t, b) for x, t, b in zip(left, through, back)]
        for block in range(4):
            to_pieces(green, out_ref, base, block)
            part = pl.ds(base + 32 * block, 32)
            sem = sems.at[8 + base // 32 + block]
            sent.append(pltpu.make_async_copy(out_ref.at[part], out_hbm.at[part], sem))
            sent[-1].start()
    for copy in sent:
        copy.wait()


def solve(sigma, ham, coupling, energies, counts):
    hbm = pl.BlockSpec(memory_space=pltpu.HBM)
    return pl.pallas_call(
        solve_kernel,
        out_shape=jax.ShapeDtypeStruct((DEVS, ROWS, 128), F32),
        in_specs=[hbm, hbm, hbm, smem(), smem()],
        out_specs=hbm,
        scratch_shapes=[
            pltpu.VMEM((DEVS, ROWS, 128), F32),
            pltpu.VMEM((PTS, 2 * M, M), F32),
            pltpu.VMEM((2 * M, M), F32),
            pltpu.VMEM((M, M), F32),
            pltpu.SemaphoreType.DMA((16,)),
        ],
        compiler_params=pltpu.CompilerParams(vmem_limit_bytes=60 * 1024 * 1024),
        cost_estimate=pl.CostEstimate(flops=6_800_000_000, bytes_accessed=5_000_000, transcendentals=0),
        name="solve_points",
    )(sigma, ham, coupling, energies, counts)


def lorentz(offset):
    scaled = offset / BROADENING
    return 1.0 / (1.0 + scaled * scaled)


def energy_operator(energies):
    columns = jnp.broadcast_to(energies, (E_TOT, E_TOT))
    spacing = columns.T - columns
    values = lorentz(spacing - PHONON) + lorentz(spacing + PHONON)
    values = values / jnp.sum(values, axis=1, keepdims=True)
    wide = E_TOT * 2
    spread = (
        lax.broadcasted_iota(jnp.int32, (wide, E_TOT), 0) // 2
        == lax.broadcasted_iota(jnp.int32, (wide, E_TOT), 1)
    ).astype(BF16)
    gather = (
        lax.broadcasted_iota(jnp.int32, (E_TOT, wide), 1) // 2
        == lax.broadcasted_iota(jnp.int32, (E_TOT, wide), 0)
    ).astype(BF16)
    row_id = lax.broadcasted_iota(jnp.int32, (wide, wide), 0)
    col_id = lax.broadcasted_iota(jnp.int32, (wide, wide), 1)
    same = ((row_id ^ col_id) & 1) == 0
    parts = []
    for part in split(values):
        tall = jnp.dot(spread, part, preferred_element_type=F32).astype(BF16)
        full = jnp.dot(tall, gather, preferred_element_type=F32)
        parts.append(jnp.where(same, full, 0.0).astype(BF16))
    return parts


def mix_momenta(given, weight):
    half = KN // 2
    total = [0.5 * (weight[s] + weight[s + half]) for s in range(half)]
    change = [0.5 * (weight[s] - weight[s + half]) for s in range(half)]
    added = [given[k] + given[k + half] for k in range(half)]
    taken = [given[k] - given[k + half] for k in range(half)]
    first, second = [], []
    for k in range(half):
        cyclic = total[0] * added[k]
        signed = change[0] * taken[k]
        for s in range(1, half):
            cyclic = cyclic + total[s] * added[(k - s) % half]
            term = change[s] * taken[(k - s) % half]
            signed = signed + term if k >= s else signed - term
        first.append(cyclic + signed)
        second.append(cyclic - signed)
    return first + second


def mix_kernel(energy_ref, strength_ref, offset_ref, in_ref, out_ref, x_high, x_low):
    weight = []
    for d in range(KN):
        total = jnp.float32(0.0)
        for j in range(16):
            total = total + jnp.where(offset_ref[j] == d, strength_ref[j], 0.0)
        weight.append(total)
    high, low = energy_operator(energy_ref[...])
    left = jnp.concatenate([high, high, low], axis=1)
    for upper in range(2):
        for device in range(16):
            given = [in_ref[(upper * KN + k) * 16 + device] for k in range(KN)]
            rows = slice((upper * 16 + device) * 8, (upper * 16 + device) * 8 + 8)
            for k, mixed in enumerate(mix_momenta(given, weight)):
                for tile, part in enumerate(split(mixed)):
                    ref = (x_high, x_low)[tile]
                    ref[rows, k * 256 : k * 256 + 128] = part[:8]
                    ref[rows, k * 256 + 128 : k * 256 + 256] = part[8:]
    for k in range(KN):
        lanes = slice(k * 256, k * 256 + 256)
        right = jnp.concatenate([x_high[:, lanes], x_low[:, lanes], x_high[:, lanes]], axis=0)
        mixed = jnp.dot(left, right, preferred_element_type=F32).reshape(32, 8, 256)
        for upper in range(2):
            part = mixed[upper * 16 : upper * 16 + 16]
            first = (upper * KN + k) * 16
            out_ref[first : first + 16, :8] = part[:, :, :128]
            out_ref[first : first + 16, 8:] = part[:, :, 128:]


def mix(energies, strengths, offsets, x):
    return pl.pallas_call(
        mix_kernel,
        out_shape=jax.ShapeDtypeStruct((DEVS, ROWS, 128), F32),
        in_specs=[vmem(), smem(), smem(), vmem()],
        out_specs=vmem(),
        scratch_shapes=[
            pltpu.VMEM((256, 2048), BF16),
            pltpu.VMEM((256, 2048), BF16),
        ],
        compiler_params=pltpu.CompilerParams(vmem_limit_bytes=32 * 1024 * 1024),
        cost_estimate=pl.CostEstimate(flops=900_000_000, bytes_accessed=4_200_000, transcendentals=0),
        name="mix_energies",
    )(energies, strengths, offsets, x)


def blend_kernel(sigma_ref, in_ref, out_hbm, out_ref, sems):
    copies = []
    for block in range(4):
        for t in range(16 * block, 16 * block + 16):
            rows = slice(8 * t, 8 * t + 8)
            for half in range(2):
                lanes = slice(half * 128, half * 128 + 128)
                even = in_ref[4 * t + half]
                odd = in_ref[4 * t + 2 + half]
                tiles = transpose_rows((even[:8], even[8:], odd[:8], odd[8:]))
                for p, tile in enumerate(tiles):
                    old = sigma_ref[p, rows, lanes]
                    out_ref[p, rows, lanes] = (1.0 - MIX_RATE) * old + MIX_RATE * tile
        rows = pl.ds(128 * block, 128)
        copies.append(
            pltpu.make_async_copy(out_ref.at[:, rows], out_hbm.at[:, rows], sems.at[block])
        )
        copies[-1].start()
    for copy in copies:
        copy.wait()


def blend(sigma, x):
    return pl.pallas_call(
        blend_kernel,
        out_shape=jax.ShapeDtypeStruct((PTS, 2 * M, M), F32),
        in_specs=[vmem(), vmem()],
        out_specs=pl.BlockSpec(memory_space=pltpu.HBM),
        scratch_shapes=[pltpu.VMEM((PTS, 2 * M, M), F32), pltpu.SemaphoreType.DMA((4,))],
        compiler_params=pltpu.CompilerParams(vmem_limit_bytes=24 * 1024 * 1024),
        cost_estimate=pl.CostEstimate(flops=2_000_000, bytes_accessed=6_000_000, transcendentals=0),
        name="blend_old",
    )(sigma, x)


def exchange(x):
    return lax.all_to_all(x, ORDER, split_axis=0, concat_axis=0, tiled=True)


def body(sigma_in, hamiltonian, coupling, energies, counts, strengths, offsets):
    sigma = sigma_in.reshape(PTS, 2 * M, M)
    green = solve(sigma, hamiltonian.reshape(2 * M, M), coupling.reshape(M, M), energies, counts)
    columns = exchange(green)
    mixed = mix(energies.reshape(1, E_TOT), strengths, offsets, columns)
    result = exchange(mixed)
    return blend(sigma, result).reshape(sigma_in.shape)


def solution(mesh):
    fine = Mesh(mesh.devices.reshape(2, 8, 2, 2, 4), ("xl", "z", "c", "xh", "y"))
    energy, mom = ("xl", "z", "c"), ("xh", "y")
    return jax.shard_map(
        body,
        mesh=fine,
        in_specs=(
            P(energy, mom, None, None, None),
            P(mom, None, None, None),
            P(mom, None, None),
            P(),
            P(),
            P(),
            P(),
        ),
        out_specs=P(energy, mom, None, None, None),
        check_vma=False,
    )
```

```python
import jax
import jax.numpy as jnp
from jax import lax
from jax.experimental import pallas as pl
from jax.experimental.pallas import tpu as pltpu
from jax.sharding import Mesh
from jax.sharding import PartitionSpec as P

MIX_RATE = 0.6
PHONON = 0.1
BROADENING = 0.02
GOLDEN = 0.5 + 0.5 * 5.0**0.5

M = 256
PTS = 4
E_TOT = 128
KN = 8
DEVS = 256
ROWS = 16
ORDER = ("xl", "xh", "y", "z", "c")
F32 = jnp.float32
BF16 = jnp.bfloat16


def vmem():
    return pl.BlockSpec(memory_space=pltpu.VMEM)


def smem():
    return pl.BlockSpec(memory_space=pltpu.SMEM)


def split(x):
    high = x.astype(BF16)
    return high, (x - high.astype(F32)).astype(BF16)


def dot3(a, b):
    left = jnp.concatenate([a[0], a[0], a[1]], axis=1)
    right = jnp.concatenate([b[0], b[1], b[0]], axis=0)
    return jnp.dot(left, right, preferred_element_type=F32)


def exchange_rows(x, y, group):
    axis = x.ndim - 2
    even = lax.broadcasted_iota(jnp.int32, x.shape, axis) // group % 2 == 0
    first = jnp.where(even, x, pltpu.roll(y, group, axis))
    second = jnp.where(even, pltpu.roll(x, 8 - group, axis), y)
    return first, second


def transpose_rows(tiles):
    a, c = exchange_rows(tiles[0], tiles[2], 4)
    b, d = exchange_rows(tiles[1], tiles[3], 4)
    return exchange_rows(a, b, 2) + exchange_rows(c, d, 2)


def invert_all(residuals, scales, slow):
    rows = lax.broadcasted_iota(jnp.int32, (M, M), 0)
    cols = lax.broadcasted_iota(jnp.int32, (M, M), 1)
    eye = (rows == cols).astype(F32)
    pairs = [split(r) for r in residuals]
    seconds = [dot3(p, p) for p in pairs]
    thirds = [dot3(split(q), p) for q, p in zip(seconds, pairs)]
    sums = [r + q + t for r, q, t in zip(residuals, seconds, thirds)]
    cubes = [split(t) for t in thirds]
    sixths = [dot3(c, c) + eye for c in cubes]
    quartics = [
        dot3(split(u + GOLDEN * t), split(u - (1.0 / GOLDEN) * t)) for u, t in zip(sixths, thirds)
    ]
    longs = [dot3(split(r), split(q)) for r, q in zip(sums, quartics)]
    return [
        (eye + jnp.where(f, x, r)) * s for f, x, r, s in zip(slow, longs, sums, scales)
    ]


def to_pieces(green, out_ref, base, block):
    slab = slice(block * 64, block * 64 + 64)
    for q, tiles in enumerate(transpose_rows([g[slab].reshape(8, 8, M) for g in green])):
        for t in range(8):
            for half in range(2):
                piece = base + block * 32 + 4 * t + 2 * (q // 2) + half
                rows = slice(q % 2 * 8, q % 2 * 8 + 8)
                out_ref[piece, rows] = tiles[t, :, half * 128 : half * 128 + 128]


def solve_kernel(
    sigma_hbm,
    ham_hbm,
    coup_hbm,
    energy_hbm,
    count_hbm,
    out_ref,
    sigma_ref,
    ham_ref,
    coup_ref,
    energy_ref,
    count_ref,
    sems,
):
    upper, lower = pl.ds(0, M), pl.ds(M, M)
    copies = [
        pltpu.make_async_copy(coup_hbm, coup_ref, sems.at[0]),
        pltpu.make_async_copy(ham_hbm.at[upper], ham_ref.at[upper], sems.at[1]),
        *(
            pltpu.make_async_copy(sigma_hbm.at[p, upper], sigma_ref.at[p, upper], sems.at[2 + p])
            for p in range(PTS)
        ),
        pltpu.make_async_copy(ham_hbm.at[lower], ham_ref.at[lower], sems.at[6]),
        pltpu.make_async_copy(sigma_hbm.at[:, lower], sigma_ref.at[:, lower], sems.at[7]),
    ]
    scalars = [
        pltpu.make_async_copy(energy_hbm, energy_ref, sems.at[16]),
        pltpu.make_async_copy(count_hbm, count_ref, sems.at[17]),
    ]
    for copy in scalars:
        copy.start()
    for copy in copies:
        copy.start()
    copies[0].wait()
    coupling = split(coup_ref[...])
    turned = split(coup_ref[...].T)
    for copy in scalars:
        copy.wait()
    rank = (lax.axis_index("xl") * 8 + lax.axis_index("z")) * 2 + lax.axis_index("c")
    points = range(PTS)
    energy = [energy_ref[rank * PTS + p] for p in points]
    slow = [count_ref[rank * PTS + p] > 2 for p in points]
    scale = [1.0 / jnp.full((1, 1), e, F32) for e in energy]
    copies[1].wait()
    residual = []
    for p in points:
        copies[2 + p].wait()
        residual.append((ham_ref[:M] + sigma_ref[p, :M]) * scale[p])
    left = invert_all(residual, scale, slow)
    for copy in copies[6:]:
        copy.wait()
    inverse = [split(x) for x in left]
    coupled = [split(dot3(x, coupling)) for x in inverse]
    back = [split(dot3(turned, x)) for x in inverse]
    residual = [
        (ham_ref[M:] + sigma_ref[p, M:] + dot3(turned, coupled[p])) * scale[p] for p in points
    ]
    right = invert_all(residual, scale, slow)
    through = [split(dot3(c, split(r))) for c, r in zip(coupled, right)]
    for base, green in ((128, right), (0, None)):
        if green is None:
            green = [x + dot3(t, b) for x, t, b in zip(left, through, back)]
        for block in range(4):
            to_pieces(green, out_ref, base, block)


def solve(sigma, ham, coupling, energies, counts):
    hbm = pl.BlockSpec(memory_space=pltpu.HBM)
    sigma, ham, coupling, energies, counts = (
        pltpu.with_memory_space_constraint(v, pltpu.HBM) for v in (sigma, ham, coupling, energies, counts)
    )
    return pl.pallas_call(
        solve_kernel,
        out_shape=jax.ShapeDtypeStruct((DEVS, ROWS, 128), F32),
        in_specs=[hbm] * 5,
        out_specs=vmem(),
        scratch_shapes=[
            pltpu.VMEM((PTS, 2 * M, M), F32),
            pltpu.VMEM((2 * M, M), F32),
            pltpu.VMEM((M, M), F32),
            pltpu.SMEM((E_TOT,), F32),
            pltpu.SMEM((E_TOT,), jnp.int32),
            pltpu.SemaphoreType.DMA((18,)),
        ],
        compiler_params=pltpu.CompilerParams(vmem_limit_bytes=40 * 1024 * 1024),
        cost_estimate=pl.CostEstimate(flops=6_800_000_000, bytes_accessed=5_000_000, transcendentals=0),
        name="solve_points",
    )(sigma, ham, coupling, energies, counts)


def lorentz(offset):
    scaled = offset / BROADENING
    return 1.0 / (1.0 + scaled * scaled)


def energy_operator(energies):
    columns = jnp.broadcast_to(energies, (E_TOT, E_TOT))
    spacing = columns.T - columns
    values = lorentz(spacing - PHONON) + lorentz(spacing + PHONON)
    values = values / jnp.sum(values, axis=1, keepdims=True)
    wide = E_TOT * 2
    spread = (
        lax.broadcasted_iota(jnp.int32, (wide, E_TOT), 0) // 2
        == lax.broadcasted_iota(jnp.int32, (wide, E_TOT), 1)
    ).astype(BF16)
    gather = (
        lax.broadcasted_iota(jnp.int32, (E_TOT, wide), 1) // 2
        == lax.broadcasted_iota(jnp.int32, (E_TOT, wide), 0)
    ).astype(BF16)
    row_id = lax.broadcasted_iota(jnp.int32, (wide, wide), 0)
    col_id = lax.broadcasted_iota(jnp.int32, (wide, wide), 1)
    same = ((row_id ^ col_id) & 1) == 0
    parts = []
    for part in split(values):
        tall = jnp.dot(spread, part, preferred_element_type=F32).astype(BF16)
        full = jnp.dot(tall, gather, preferred_element_type=F32)
        parts.append(jnp.where(same, full, 0.0).astype(BF16))
    return parts


def mix_momenta(given, weight):
    half = KN // 2
    total = [0.5 * (weight[s] + weight[s + half]) for s in range(half)]
    change = [0.5 * (weight[s] - weight[s + half]) for s in range(half)]
    added = [given[k] + given[k + half] for k in range(half)]
    taken = [given[k] - given[k + half] for k in range(half)]
    first, second = [], []
    for k in range(half):
        cyclic = total[0] * added[k]
        signed = change[0] * taken[k]
        for s in range(1, half):
            cyclic = cyclic + total[s] * added[(k - s) % half]
            term = change[s] * taken[(k - s) % half]
            signed = signed + term if k >= s else signed - term
        first.append(cyclic + signed)
        second.append(cyclic - signed)
    return first + second


def mix_kernel(energy_ref, strength_ref, offset_ref, in_ref, out_ref, x_high, x_low):
    weight = []
    for d in range(KN):
        total = jnp.float32(0.0)
        for j in range(16):
            total = total + jnp.where(offset_ref[j] == d, strength_ref[j], 0.0)
        weight.append(total)
    high, low = energy_operator(energy_ref[...])
    left = jnp.concatenate([high, high, low], axis=1)
    for upper in range(2):
        for device in range(16):
            given = [in_ref[(upper * KN + k) * 16 + device] for k in range(KN)]
            rows = slice((upper * 16 + device) * 8, (upper * 16 + device) * 8 + 8)
            for k, mixed in enumerate(mix_momenta(given, weight)):
                for tile, part in enumerate(split(mixed)):
                    ref = (x_high, x_low)[tile]
                    ref[rows, k * 256 : k * 256 + 128] = part[:8]
                    ref[rows, k * 256 + 128 : k * 256 + 256] = part[8:]
    for k in range(KN):
        lanes = slice(k * 256, k * 256 + 256)
        right = jnp.concatenate([x_high[:, lanes], x_low[:, lanes], x_high[:, lanes]], axis=0)
        mixed = jnp.dot(left, right, preferred_element_type=F32).reshape(32, 8, 256)
        for upper in range(2):
            part = mixed[upper * 16 : upper * 16 + 16]
            first = (upper * KN + k) * 16
            out_ref[first : first + 16, :8] = part[:, :, :128]
            out_ref[first : first + 16, 8:] = part[:, :, 128:]


def mix(energies, strengths, offsets, x):
    return pl.pallas_call(
        mix_kernel,
        out_shape=jax.ShapeDtypeStruct((DEVS, ROWS, 128), F32),
        in_specs=[vmem(), smem(), smem(), vmem()],
        out_specs=vmem(),
        scratch_shapes=[
            pltpu.VMEM((256, 2048), BF16),
            pltpu.VMEM((256, 2048), BF16),
        ],
        compiler_params=pltpu.CompilerParams(vmem_limit_bytes=32 * 1024 * 1024),
        cost_estimate=pl.CostEstimate(flops=900_000_000, bytes_accessed=4_200_000, transcendentals=0),
        name="mix_energies",
    )(energies, strengths, offsets, x)


def blend_kernel(sigma_ref, in_ref, out_hbm, out_ref, sems):
    copies = []
    for block in range(4):
        for t in range(16 * block, 16 * block + 16):
            rows = slice(8 * t, 8 * t + 8)
            for half in range(2):
                lanes = slice(half * 128, half * 128 + 128)
                even = in_ref[4 * t + half]
                odd = in_ref[4 * t + 2 + half]
                tiles = transpose_rows((even[:8], even[8:], odd[:8], odd[8:]))
                for p, tile in enumerate(tiles):
                    old = sigma_ref[p, rows, lanes]
                    out_ref[p, rows, lanes] = (1.0 - MIX_RATE) * old + MIX_RATE * tile
        rows = pl.ds(128 * block, 128)
        copies.append(
            pltpu.make_async_copy(out_ref.at[:, rows], out_hbm.at[:, rows], sems.at[block])
        )
        copies[-1].start()
    for copy in copies:
        copy.wait()


def blend(sigma, x):
    return pl.pallas_call(
        blend_kernel,
        out_shape=jax.ShapeDtypeStruct((PTS, 2 * M, M), F32),
        in_specs=[vmem(), vmem()],
        out_specs=pl.BlockSpec(memory_space=pltpu.HBM),
        scratch_shapes=[pltpu.VMEM((PTS, 2 * M, M), F32), pltpu.SemaphoreType.DMA((4,))],
        compiler_params=pltpu.CompilerParams(vmem_limit_bytes=24 * 1024 * 1024),
        cost_estimate=pl.CostEstimate(flops=2_000_000, bytes_accessed=6_000_000, transcendentals=0),
        name="blend_old",
    )(sigma, x)


def exchange(x):
    return lax.all_to_all(x, ORDER, split_axis=0, concat_axis=0, tiled=True)


def body(sigma_in, hamiltonian, coupling, energies, counts, strengths, offsets):
    sigma = sigma_in.reshape(PTS, 2 * M, M)
    green = solve(sigma, hamiltonian.reshape(2 * M, M), coupling.reshape(M, M), energies, counts)
    columns = exchange(green)
    mixed = mix(energies.reshape(1, E_TOT), strengths, offsets, columns)
    result = exchange(mixed)
    return blend(sigma, result).reshape(sigma_in.shape)


def solution(mesh):
    fine = Mesh(mesh.devices.reshape(2, 8, 2, 2, 4), ("xl", "z", "c", "xh", "y"))
    energy, mom = ("xl", "z", "c"), ("xh", "y")
    return jax.shard_map(
        body,
        mesh=fine,
        in_specs=(
            P(energy, mom, None, None, None),
            P(mom, None, None, None),
            P(mom, None, None),
            P(),
            P(),
            P(),
            P(),
        ),
        out_specs=P(energy, mom, None, None, None),
        check_vma=False,
    )
```

```python
import jax
import jax.numpy as jnp
from jax import lax
from jax.experimental import pallas as pl
from jax.experimental.pallas import tpu as pltpu
from jax.sharding import Mesh
from jax.sharding import PartitionSpec as P

MIX_RATE = 0.6
PHONON = 0.1
BROADENING = 0.02
GOLDEN = 0.5 + 0.5 * 5.0**0.5

M = 256
PTS = 4
E_TOT = 128
KN = 8
DEVS = 256
ROWS = 16
ORDER = ("xl", "xh", "y", "z", "c")
F32 = jnp.float32
BF16 = jnp.bfloat16


def vmem():
    return pl.BlockSpec(memory_space=pltpu.VMEM)


def split(x):
    high = x.astype(BF16)
    return high, (x - high.astype(F32)).astype(BF16)


def dot3(a, b):
    left = jnp.concatenate([a[0], a[0], a[1]], axis=1)
    right = jnp.concatenate([b[0], b[1], b[0]], axis=0)
    return jnp.dot(left, right, preferred_element_type=F32)


def exchange_rows(x, y, group):
    axis = x.ndim - 2
    even = lax.broadcasted_iota(jnp.int32, x.shape, axis) // group % 2 == 0
    first = jnp.where(even, x, pltpu.roll(y, group, axis))
    second = jnp.where(even, pltpu.roll(x, 8 - group, axis), y)
    return first, second


def transpose_rows(tiles):
    a, c = exchange_rows(tiles[0], tiles[2], 4)
    b, d = exchange_rows(tiles[1], tiles[3], 4)
    return exchange_rows(a, b, 2) + exchange_rows(c, d, 2)


def invert_all(residuals, scales, slow):
    rows = lax.broadcasted_iota(jnp.int32, (M, M), 0)
    cols = lax.broadcasted_iota(jnp.int32, (M, M), 1)
    eye = (rows == cols).astype(F32)
    pairs = [split(r) for r in residuals]
    seconds = [dot3(p, p) for p in pairs]
    thirds = [dot3(split(q), p) for q, p in zip(seconds, pairs)]
    sums = [r + q + t for r, q, t in zip(residuals, seconds, thirds)]
    cubes = [split(t) for t in thirds]
    sixths = [dot3(c, c) + eye for c in cubes]
    quartics = [
        dot3(split(u + GOLDEN * t), split(u - (1.0 / GOLDEN) * t)) for u, t in zip(sixths, thirds)
    ]
    longs = [dot3(split(r), split(q)) for r, q in zip(sums, quartics)]
    return [
        (eye + jnp.where(f, x, r)) * s for f, x, r, s in zip(slow, longs, sums, scales)
    ]


def to_pieces(green, out_ref, base, block):
    slab = slice(block * 64, block * 64 + 64)
    for q, tiles in enumerate(transpose_rows([g[slab].reshape(8, 8, M) for g in green])):
        for t in range(8):
            for half in range(2):
                piece = base + block * 32 + 4 * t + 2 * (q // 2) + half
                rows = slice(q % 2 * 8, q % 2 * 8 + 8)
                out_ref[piece, rows] = tiles[t, :, half * 128 : half * 128 + 128]


def solve_kernel(
    sigma_hbm,
    ham_hbm,
    coup_hbm,
    energy_hbm,
    count_hbm,
    out_ref,
    sigma_ref,
    ham_ref,
    coup_ref,
    energy_ref,
    count_ref,
    sems,
):
    upper, lower = pl.ds(0, M), pl.ds(M, M)
    copies = [
        pltpu.make_async_copy(coup_hbm, coup_ref, sems.at[0]),
        pltpu.make_async_copy(ham_hbm.at[upper], ham_ref.at[upper], sems.at[1]),
        *(
            pltpu.make_async_copy(sigma_hbm.at[p, upper], sigma_ref.at[p, upper], sems.at[2 + p])
            for p in range(PTS)
        ),
        pltpu.make_async_copy(ham_hbm.at[lower], ham_ref.at[lower], sems.at[6]),
        pltpu.make_async_copy(sigma_hbm.at[:, lower], sigma_ref.at[:, lower], sems.at[7]),
    ]
    scalars = [
        pltpu.make_async_copy(energy_hbm, energy_ref, sems.at[16]),
        pltpu.make_async_copy(count_hbm, count_ref, sems.at[17]),
    ]
    for copy in scalars:
        copy.start()
    for copy in copies:
        copy.start()
    copies[0].wait()
    coupling = split(coup_ref[...])
    turned = split(coup_ref[...].T)
    for copy in scalars:
        copy.wait()
    rank = (lax.axis_index("xl") * 8 + lax.axis_index("z")) * 2 + lax.axis_index("c")
    points = range(PTS)
    energy = [energy_ref[rank * PTS + p] for p in points]
    slow = [count_ref[rank * PTS + p] > 2 for p in points]
    scale = [1.0 / jnp.full((1, 1), e, F32) for e in energy]
    copies[1].wait()
    residual = []
    for p in points:
        copies[2 + p].wait()
        residual.append((ham_ref[:M] + sigma_ref[p, :M]) * scale[p])
    left = invert_all(residual, scale, slow)
    for copy in copies[6:]:
        copy.wait()
    inverse = [split(x) for x in left]
    coupled = [split(dot3(x, coupling)) for x in inverse]
    back = [split(dot3(turned, x)) for x in inverse]
    residual = [
        (ham_ref[M:] + sigma_ref[p, M:] + dot3(turned, coupled[p])) * scale[p] for p in points
    ]
    right = invert_all(residual, scale, slow)
    through = [split(dot3(c, split(r))) for c, r in zip(coupled, right)]
    for base, green in ((128, right), (0, None)):
        if green is None:
            green = [x + dot3(t, b) for x, t, b in zip(left, through, back)]
        for block in range(4):
            to_pieces(green, out_ref, base, block)


def solve(sigma, ham, coupling, energies, counts):
    hbm = pl.BlockSpec(memory_space=pltpu.HBM)
    sigma, ham, coupling, energies, counts = (
        pltpu.with_memory_space_constraint(v, pltpu.HBM) for v in (sigma, ham, coupling, energies, counts)
    )
    return pl.pallas_call(
        solve_kernel,
        out_shape=jax.ShapeDtypeStruct((DEVS, ROWS, 128), F32),
        in_specs=[hbm] * 5,
        out_specs=vmem(),
        scratch_shapes=[
            pltpu.VMEM((PTS, 2 * M, M), F32),
            pltpu.VMEM((2 * M, M), F32),
            pltpu.VMEM((M, M), F32),
            pltpu.SMEM((E_TOT,), F32),
            pltpu.SMEM((E_TOT,), jnp.int32),
            pltpu.SemaphoreType.DMA((18,)),
        ],
        compiler_params=pltpu.CompilerParams(vmem_limit_bytes=40 * 1024 * 1024),
        cost_estimate=pl.CostEstimate(flops=6_800_000_000, bytes_accessed=5_000_000, transcendentals=0),
        name="solve_points",
    )(sigma, ham, coupling, energies, counts)


def lorentz(offset):
    scaled = offset / BROADENING
    return 1.0 / (1.0 + scaled * scaled)


def energy_operator(energies):
    columns = jnp.broadcast_to(energies, (E_TOT, E_TOT))
    spacing = columns.T - columns
    values = lorentz(spacing - PHONON) + lorentz(spacing + PHONON)
    values = values / jnp.sum(values, axis=1, keepdims=True)
    wide = E_TOT * 2
    spread = (
        lax.broadcasted_iota(jnp.int32, (wide, E_TOT), 0) // 2
        == lax.broadcasted_iota(jnp.int32, (wide, E_TOT), 1)
    ).astype(BF16)
    gather = (
        lax.broadcasted_iota(jnp.int32, (E_TOT, wide), 1) // 2
        == lax.broadcasted_iota(jnp.int32, (E_TOT, wide), 0)
    ).astype(BF16)
    row_id = lax.broadcasted_iota(jnp.int32, (wide, wide), 0)
    col_id = lax.broadcasted_iota(jnp.int32, (wide, wide), 1)
    same = ((row_id ^ col_id) & 1) == 0
    parts = []
    for part in split(values):
        tall = jnp.dot(spread, part, preferred_element_type=F32).astype(BF16)
        full = jnp.dot(tall, gather, preferred_element_type=F32)
        parts.append(jnp.where(same, full, 0.0).astype(BF16))
    return parts


def mix_momenta(given, weight):
    half = KN // 2
    total, change = weight
    added = [given[k] + given[k + half] for k in range(half)]
    taken = [given[k] - given[k + half] for k in range(half)]
    first, second = [], []
    for k in range(half):
        cyclic = total[0] * added[k]
        signed = change[0] * taken[k]
        for s in range(1, half):
            cyclic = cyclic + total[s] * added[(k - s) % half]
            term = change[s] * taken[(k - s) % half]
            signed = signed + term if k >= s else signed - term
        first.append(cyclic + signed)
        second.append(cyclic - signed)
    return first + second


def mix_kernel(energy_ref, strength_ref, offset_ref, in_ref, out_ref, x_high, x_low):
    weight = []
    for d in range(KN):
        chosen = jnp.where(offset_ref[...] == d, strength_ref[...], 0.0)
        weight.append(jnp.sum(chosen, axis=1, keepdims=True))
    half = KN // 2
    halves = [
        [jnp.broadcast_to(0.5 * (weight[s] + sign * weight[s + half]), (ROWS, 128)) for s in range(half)]
        for sign in (1.0, -1.0)
    ]
    high, low = energy_operator(energy_ref[...])
    left = jnp.concatenate([high, high, low], axis=1)
    for upper in range(2):
        for device in range(16):
            given = [in_ref[(upper * KN + k) * 16 + device] for k in range(KN)]
            rows = slice((upper * 16 + device) * 8, (upper * 16 + device) * 8 + 8)
            for k, mixed in enumerate(mix_momenta(given, halves)):
                for tile, part in enumerate(split(mixed)):
                    ref = (x_high, x_low)[tile]
                    ref[rows, k * 256 : k * 256 + 128] = part[:8]
                    ref[rows, k * 256 + 128 : k * 256 + 256] = part[8:]
    for k in range(KN):
        lanes = slice(k * 256, k * 256 + 256)
        right = jnp.concatenate([x_high[:, lanes], x_low[:, lanes], x_high[:, lanes]], axis=0)
        mixed = jnp.dot(left, right, preferred_element_type=F32).reshape(32, 8, 256)
        for upper in range(2):
            part = mixed[upper * 16 : upper * 16 + 16]
            first = (upper * KN + k) * 16
            out_ref[first : first + 16, :8] = part[:, :, :128]
            out_ref[first : first + 16, 8:] = part[:, :, 128:]


def mix(energies, strengths, offsets, x):
    return pl.pallas_call(
        mix_kernel,
        out_shape=jax.ShapeDtypeStruct((DEVS, ROWS, 128), F32),
        in_specs=[vmem()] * 4,
        out_specs=vmem(),
        scratch_shapes=[
            pltpu.VMEM((256, 2048), BF16),
            pltpu.VMEM((256, 2048), BF16),
        ],
        compiler_params=pltpu.CompilerParams(vmem_limit_bytes=32 * 1024 * 1024),
        cost_estimate=pl.CostEstimate(flops=900_000_000, bytes_accessed=4_200_000, transcendentals=0),
        name="mix_energies",
    )(energies, strengths, offsets, x)


def blend_kernel(sigma_ref, in_ref, out_hbm, out_ref, sems):
    copies = []
    for block in range(4):
        for t in range(16 * block, 16 * block + 16):
            rows = slice(8 * t, 8 * t + 8)
            for half in range(2):
                lanes = slice(half * 128, half * 128 + 128)
                even = in_ref[4 * t + half]
                odd = in_ref[4 * t + 2 + half]
                tiles = transpose_rows((even[:8], even[8:], odd[:8], odd[8:]))
                for p, tile in enumerate(tiles):
                    old = sigma_ref[p, rows, lanes]
                    out_ref[p, rows, lanes] = (1.0 - MIX_RATE) * old + MIX_RATE * tile
        rows = pl.ds(128 * block, 128)
        copies.append(
            pltpu.make_async_copy(out_ref.at[:, rows], out_hbm.at[:, rows], sems.at[block])
        )
        copies[-1].start()
    for copy in copies:
        copy.wait()


def blend(sigma, x):
    return pl.pallas_call(
        blend_kernel,
        out_shape=jax.ShapeDtypeStruct((PTS, 2 * M, M), F32),
        in_specs=[vmem(), vmem()],
        out_specs=pl.BlockSpec(memory_space=pltpu.HBM),
        scratch_shapes=[pltpu.VMEM((PTS, 2 * M, M), F32), pltpu.SemaphoreType.DMA((4,))],
        compiler_params=pltpu.CompilerParams(vmem_limit_bytes=24 * 1024 * 1024),
        cost_estimate=pl.CostEstimate(flops=2_000_000, bytes_accessed=6_000_000, transcendentals=0),
        name="blend_old",
    )(sigma, x)


def exchange(x):
    return lax.all_to_all(x, ORDER, split_axis=0, concat_axis=0, tiled=True)


def body(sigma_in, hamiltonian, coupling, energies, counts, strengths, offsets):
    sigma = sigma_in.reshape(PTS, 2 * M, M)
    green = solve(sigma, hamiltonian.reshape(2 * M, M), coupling.reshape(M, M), energies, counts)
    columns = exchange(green)
    mixed = mix(energies.reshape(1, -1), strengths.reshape(1, -1), offsets.reshape(1, -1), columns)
    result = exchange(mixed)
    return blend(sigma, result).reshape(sigma_in.shape)


def solution(mesh):
    fine = Mesh(mesh.devices.reshape(2, 8, 2, 2, 4), ("xl", "z", "c", "xh", "y"))
    energy, mom = ("xl", "z", "c"), ("xh", "y")
    return jax.shard_map(
        body,
        mesh=fine,
        in_specs=(
            P(energy, mom, None, None, None),
            P(mom, None, None, None),
            P(mom, None, None),
            P(),
            P(),
            P(),
            P(),
        ),
        out_specs=P(energy, mom, None, None, None),
        check_vma=False,
    )
```

```python
import jax
import jax.numpy as jnp
from jax import lax
from jax.experimental import pallas as pl
from jax.experimental.pallas import tpu as pltpu
from jax.sharding import Mesh
from jax.sharding import PartitionSpec as P

MIX_RATE = 0.6
PHONON = 0.1
BROADENING = 0.02
GOLDEN = 0.5 + 0.5 * 5.0**0.5

M = 256
PTS = 4
E_TOT = 128
KN = 8
CHIPS = 128
ROWS = 32
ORDER = ("xl", "xh", "y", "z")
F32 = jnp.float32
BF16 = jnp.bfloat16


def vmem():
    return pl.BlockSpec(memory_space=pltpu.VMEM)


def split(x):
    high = x.astype(BF16)
    return high, (x - high.astype(F32)).astype(BF16)


def dot3(a, b):
    left = jnp.concatenate([a[0], a[0], a[1]], axis=1)
    right = jnp.concatenate([b[0], b[1], b[0]], axis=0)
    return jnp.dot(left, right, preferred_element_type=F32)


def exchange_rows(x, y, group):
    axis = x.ndim - 2
    even = lax.broadcasted_iota(jnp.int32, x.shape, axis) // group % 2 == 0
    first = jnp.where(even, x, pltpu.roll(y, group, axis))
    second = jnp.where(even, pltpu.roll(x, 8 - group, axis), y)
    return first, second


def transpose_rows(tiles):
    a, c = exchange_rows(tiles[0], tiles[2], 4)
    b, d = exchange_rows(tiles[1], tiles[3], 4)
    return exchange_rows(a, b, 2) + exchange_rows(c, d, 2)


def invert_all(residuals, scales, slow):
    rows = lax.broadcasted_iota(jnp.int32, (M, M), 0)
    cols = lax.broadcasted_iota(jnp.int32, (M, M), 1)
    eye = (rows == cols).astype(F32)
    pairs = [split(r) for r in residuals]
    seconds = [dot3(p, p) for p in pairs]
    thirds = [dot3(split(q), p) for q, p in zip(seconds, pairs)]
    sums = [r + q + t for r, q, t in zip(residuals, seconds, thirds)]
    cubes = [split(t) for t in thirds]
    sixths = [dot3(c, c) + eye for c in cubes]
    quartics = [
        dot3(split(u + GOLDEN * t), split(u - (1.0 / GOLDEN) * t)) for u, t in zip(sixths, thirds)
    ]
    longs = [dot3(split(r), split(q)) for r, q in zip(sums, quartics)]
    return [
        (eye + jnp.where(f, x, r)) * s for f, x, r, s in zip(slow, longs, sums, scales)
    ]


def to_pieces(green, out_ref, base, block):
    slab = slice(block * 64, block * 64 + 64)
    for q, tiles in enumerate(transpose_rows([g[slab].reshape(8, 8, M) for g in green])):
        for t in range(8):
            for half in range(2):
                piece = base + block * 16 + 2 * t + half
                out_ref[piece, q * 8 : q * 8 + 8] = tiles[t, :, half * 128 : half * 128 + 128]


def solve_kernel(
    sigma_hbm,
    ham_hbm,
    coup_hbm,
    energy_hbm,
    count_hbm,
    out_ref,
    sigma_ref,
    ham_ref,
    coup_ref,
    energy_ref,
    count_ref,
    sems,
):
    upper, lower = pl.ds(0, M), pl.ds(M, M)
    copies = [
        pltpu.make_async_copy(coup_hbm, coup_ref, sems.at[0]),
        pltpu.make_async_copy(ham_hbm.at[upper], ham_ref.at[upper], sems.at[1]),
        *(
            pltpu.make_async_copy(sigma_hbm.at[p, upper], sigma_ref.at[p, upper], sems.at[2 + p])
            for p in range(PTS)
        ),
        pltpu.make_async_copy(ham_hbm.at[lower], ham_ref.at[lower], sems.at[6]),
        pltpu.make_async_copy(sigma_hbm.at[:, lower], sigma_ref.at[:, lower], sems.at[7]),
    ]
    scalars = [
        pltpu.make_async_copy(energy_hbm, energy_ref, sems.at[16]),
        pltpu.make_async_copy(count_hbm, count_ref, sems.at[17]),
    ]
    for copy in scalars:
        copy.start()
    for copy in copies:
        copy.start()
    copies[0].wait()
    coupling = split(coup_ref[...])
    turned = split(coup_ref[...].T)
    for copy in scalars:
        copy.wait()
    rank = (lax.axis_index("xl") * 8 + lax.axis_index("z")) * 2 + lax.axis_index("c")
    points = range(PTS)
    energy = [energy_ref[rank * PTS + p] for p in points]
    slow = [count_ref[rank * PTS + p] > 2 for p in points]
    scale = [1.0 / jnp.full((1, 1), e, F32) for e in energy]
    copies[1].wait()
    residual = []
    for p in points:
        copies[2 + p].wait()
        residual.append((ham_ref[:M] + sigma_ref[p, :M]) * scale[p])
    left = invert_all(residual, scale, slow)
    for copy in copies[6:]:
        copy.wait()
    inverse = [split(x) for x in left]
    coupled = [split(dot3(x, coupling)) for x in inverse]
    back = [split(dot3(turned, x)) for x in inverse]
    residual = [
        (ham_ref[M:] + sigma_ref[p, M:] + dot3(turned, coupled[p])) * scale[p] for p in points
    ]
    right = invert_all(residual, scale, slow)
    through = [split(dot3(c, split(r))) for c, r in zip(coupled, right)]
    for base, green in ((64, right), (0, None)):
        if green is None:
            green = [x + dot3(t, b) for x, t, b in zip(left, through, back)]
        for block in range(4):
            to_pieces(green, out_ref, base, block)


def solve(sigma, ham, coupling, energies, counts):
    hbm = pl.BlockSpec(memory_space=pltpu.HBM)
    sigma, ham, coupling, energies, counts = (
        pltpu.with_memory_space_constraint(v, pltpu.HBM) for v in (sigma, ham, coupling, energies, counts)
    )
    return pl.pallas_call(
        solve_kernel,
        out_shape=jax.ShapeDtypeStruct((CHIPS, ROWS, 128), F32),
        in_specs=[hbm] * 5,
        out_specs=vmem(),
        scratch_shapes=[
            pltpu.VMEM((PTS, 2 * M, M), F32),
            pltpu.VMEM((2 * M, M), F32),
            pltpu.VMEM((M, M), F32),
            pltpu.SMEM((E_TOT,), F32),
            pltpu.SMEM((E_TOT,), jnp.int32),
            pltpu.SemaphoreType.DMA((18,)),
        ],
        compiler_params=pltpu.CompilerParams(vmem_limit_bytes=40 * 1024 * 1024),
        cost_estimate=pl.CostEstimate(flops=6_800_000_000, bytes_accessed=5_000_000, transcendentals=0),
        name="solve_points",
    )(sigma, ham, coupling, energies, counts)


def lorentz(offset):
    scaled = offset / BROADENING
    return 1.0 / (1.0 + scaled * scaled)


def energy_operator(energies, core):
    columns = jnp.broadcast_to(energies, (E_TOT, E_TOT))
    spacing = columns.T - columns
    values = lorentz(spacing - PHONON) + lorentz(spacing + PHONON)
    values = values / jnp.sum(values, axis=1, keepdims=True)
    wide = E_TOT
    row_id = lax.broadcasted_iota(jnp.int32, (2 * wide, E_TOT), 0)
    row_core = jnp.where(row_id < wide, core, 1 - core)
    local = row_id & (wide - 1)
    wanted = (local // 8) * 8 + row_core * 4 + (local & 7) // 2
    spread = (lax.broadcasted_iota(jnp.int32, (2 * wide, E_TOT), 1) == wanted).astype(BF16)
    col_id = lax.broadcasted_iota(jnp.int32, (E_TOT, wide), 1)
    wanted = (col_id // 8) * 8 + core * 4 + (col_id & 7) // 2
    gather = (lax.broadcasted_iota(jnp.int32, (E_TOT, wide), 0) == wanted).astype(BF16)
    row_id = lax.broadcasted_iota(jnp.int32, (2 * wide, wide), 0)
    col_id = lax.broadcasted_iota(jnp.int32, (2 * wide, wide), 1)
    same = ((row_id ^ col_id) & 1) == 0
    parts = []
    for part in split(values):
        tall = jnp.dot(spread, part, preferred_element_type=F32).astype(BF16)
        full = jnp.dot(tall, gather, preferred_element_type=F32)
        parts.append(jnp.where(same, full, 0.0).astype(BF16))
    return parts


def mix_momenta(given, weight):
    half = KN // 2
    total, change = weight
    added = [given[k] + given[k + half] for k in range(half)]
    taken = [given[k] - given[k + half] for k in range(half)]
    first, second = [], []
    for k in range(half):
        cyclic = total[0] * added[k]
        signed = change[0] * taken[k]
        for s in range(1, half):
            cyclic = cyclic + total[s] * added[(k - s) % half]
            term = change[s] * taken[(k - s) % half]
            signed = signed + term if k >= s else signed - term
        first.append(cyclic + signed)
        second.append(cyclic - signed)
    return first + second


def mix_kernel(
    energy_ref, strength_ref, offset_ref, in_ref, own_ref, first_ref, second_ref, x_high, x_low
):
    weight = []
    for d in range(KN):
        chosen = jnp.where(offset_ref[...] == d, strength_ref[...], 0.0)
        weight.append(jnp.sum(chosen, axis=1, keepdims=True))
    half = KN // 2
    halves = [
        [jnp.broadcast_to(0.5 * (weight[s] + sign * weight[s + half]), (ROWS, 128)) for s in range(half)]
        for sign in (1.0, -1.0)
    ]
    high, low = energy_operator(energy_ref[...], lax.axis_index("c"))
    left = jnp.concatenate([high, high, low], axis=1)
    for upper in range(2):
        for z in range(8):
            given = [in_ref[(upper * KN + k) * 8 + z] for k in range(KN)]
            rows = slice((upper * 8 + z) * 8, (upper * 8 + z) * 8 + 8)
            for k, mixed in enumerate(mix_momenta(given, halves)):
                for ref, part in zip((x_high, x_low), split(mixed)):
                    for q in range(4):
                        lanes = slice((4 * k + q) * 128, (4 * k + q) * 128 + 128)
                        ref[rows, lanes] = part[8 * q : 8 * q + 8]
    for k in range(KN):
        for pair, other_ref in enumerate((first_ref, second_ref)):
            lanes = slice((2 * k + pair) * 256, (2 * k + pair) * 256 + 256)
            right = jnp.concatenate([x_high[:, lanes], x_low[:, lanes], x_high[:, lanes]], axis=0)
            mixed = jnp.dot(left, right, preferred_element_type=F32).reshape(32, 8, 256)
            for upper in range(2):
                own = mixed[upper * 8 : upper * 8 + 8]
                other = mixed[16 + upper * 8 : 24 + upper * 8]
                pieces = slice((upper * KN + k) * 8, (upper * KN + k) * 8 + 8)
                for q in range(2):
                    columns = slice(q * 128, q * 128 + 128)
                    row = 16 * pair + 8 * q
                    own_ref[pieces, row : row + 8] = own[:, :, columns]
                    other_ref[pieces, 8 * q : 8 * q + 8] = other[:, :, columns]


def mix(energies, strengths, offsets, x):
    return pl.pallas_call(
        mix_kernel,
        out_shape=[
            jax.ShapeDtypeStruct((CHIPS, ROWS, 128), F32),
            jax.ShapeDtypeStruct((CHIPS, ROWS // 2, 128), F32),
            jax.ShapeDtypeStruct((CHIPS, ROWS // 2, 128), F32),
        ],
        in_specs=[vmem()] * 4,
        out_specs=[vmem()] * 3,
        scratch_shapes=[pltpu.VMEM((128, 4096), BF16), pltpu.VMEM((128, 4096), BF16)],
        compiler_params=pltpu.CompilerParams(vmem_limit_bytes=32 * 1024 * 1024),
        cost_estimate=pl.CostEstimate(flops=900_000_000, bytes_accessed=6_200_000, transcendentals=0),
        name="mix_energies",
    )(energies, strengths, offsets, x)


def add_kernel(own_ref, first_ref, second_ref, out_ref):
    out_ref[:, : ROWS // 2] = own_ref[:, : ROWS // 2] + first_ref[...]
    out_ref[:, ROWS // 2 :] = own_ref[:, ROWS // 2 :] + second_ref[...]


def add_halves(own, first, second):
    return pl.pallas_call(
        add_kernel,
        out_shape=jax.ShapeDtypeStruct((CHIPS, ROWS, 128), F32),
        in_specs=[vmem()] * 3,
        out_specs=vmem(),
        compiler_params=pltpu.CompilerParams(vmem_limit_bytes=32 * 1024 * 1024),
        cost_estimate=pl.CostEstimate(flops=600_000, bytes_accessed=6_200_000, transcendentals=0),
        name="add_halves",
    )(own, first, second)


def mix_in_chip(energies, strengths, offsets, x):
    own, first, second = mix(energies, strengths, offsets, x)
    swap = [(0, 1), (1, 0)]
    return add_halves(own, lax.ppermute(first, "c", swap), lax.ppermute(second, "c", swap))


def blend_kernel(sigma_ref, in_ref, out_hbm, out_ref, sems):
    copies = []
    for block in range(4):
        for t in range(16 * block, 16 * block + 16):
            rows = slice(8 * t, 8 * t + 8)
            for half in range(2):
                lanes = slice(half * 128, half * 128 + 128)
                piece = in_ref[2 * t + half]
                tiles = transpose_rows([piece[8 * q : 8 * q + 8] for q in range(4)])
                for p, tile in enumerate(tiles):
                    old = sigma_ref[p, rows, lanes]
                    out_ref[p, rows, lanes] = (1.0 - MIX_RATE) * old + MIX_RATE * tile
        rows = pl.ds(128 * block, 128)
        copies.append(
            pltpu.make_async_copy(out_ref.at[:, rows], out_hbm.at[:, rows], sems.at[block])
        )
        copies[-1].start()
    for copy in copies:
        copy.wait()


def blend(sigma, x):
    return pl.pallas_call(
        blend_kernel,
        out_shape=jax.ShapeDtypeStruct((PTS, 2 * M, M), F32),
        in_specs=[vmem(), vmem()],
        out_specs=pl.BlockSpec(memory_space=pltpu.HBM),
        scratch_shapes=[pltpu.VMEM((PTS, 2 * M, M), F32), pltpu.SemaphoreType.DMA((4,))],
        compiler_params=pltpu.CompilerParams(vmem_limit_bytes=24 * 1024 * 1024),
        cost_estimate=pl.CostEstimate(flops=2_000_000, bytes_accessed=6_000_000, transcendentals=0),
        name="blend_old",
    )(sigma, x)


def exchange(x):
    return lax.all_to_all(x, ORDER, split_axis=0, concat_axis=0, tiled=True)


def body(sigma_in, hamiltonian, coupling, energies, counts, strengths, offsets):
    sigma = sigma_in.reshape(PTS, 2 * M, M)
    green = solve(sigma, hamiltonian.reshape(2 * M, M), coupling.reshape(M, M), energies, counts)
    columns = exchange(green)
    mixed = mix_in_chip(
        energies.reshape(1, -1), strengths.reshape(1, -1), offsets.reshape(1, -1), columns
    )
    result = exchange(mixed)
    return blend(sigma, result).reshape(sigma_in.shape)


def solution(mesh):
    fine = Mesh(mesh.devices.reshape(2, 8, 2, 2, 4), ("xl", "z", "c", "xh", "y"))
    energy, mom = ("xl", "z", "c"), ("xh", "y")
    return jax.shard_map(
        body,
        mesh=fine,
        in_specs=(
            P(energy, mom, None, None, None),
            P(mom, None, None, None),
            P(mom, None, None),
            P(),
            P(),
            P(),
            P(),
        ),
        out_specs=P(energy, mom, None, None, None),
        check_vma=False,
    )
```

```python
import jax
import jax.numpy as jnp
from jax import lax
from jax.experimental import pallas as pl
from jax.experimental.pallas import tpu as pltpu
from jax.sharding import Mesh
from jax.sharding import PartitionSpec as P

MIX_RATE = 0.6
PHONON = 0.1
BROADENING = 0.02
GOLDEN = 0.5 + 0.5 * 5.0**0.5

M = 256
PTS = 4
E_TOT = 128
KN = 8
DEVS = 256
ROWS = 16
ORDER = ("xl", "xh", "y", "z", "c")
F32 = jnp.float32
BF16 = jnp.bfloat16


def vmem():
    return pl.BlockSpec(memory_space=pltpu.VMEM)


def split(x):
    high = x.astype(BF16)
    return high, (x - high.astype(F32)).astype(BF16)


def dot3(a, b):
    left = jnp.concatenate([a[0], a[0], a[1]], axis=1)
    right = jnp.concatenate([b[0], b[1], b[0]], axis=0)
    return jnp.dot(left, right, preferred_element_type=F32)


def exchange_rows(x, y, group):
    axis = x.ndim - 2
    even = lax.broadcasted_iota(jnp.int32, x.shape, axis) // group % 2 == 0
    first = jnp.where(even, x, pltpu.roll(y, group, axis))
    second = jnp.where(even, pltpu.roll(x, 8 - group, axis), y)
    return first, second


def transpose_rows(tiles):
    a, c = exchange_rows(tiles[0], tiles[2], 4)
    b, d = exchange_rows(tiles[1], tiles[3], 4)
    return exchange_rows(a, b, 2) + exchange_rows(c, d, 2)


def invert_all(residuals, scales, slow):
    rows = lax.broadcasted_iota(jnp.int32, (M, M), 0)
    cols = lax.broadcasted_iota(jnp.int32, (M, M), 1)
    eye = (rows == cols).astype(F32)
    pairs = [split(r) for r in residuals]
    seconds = [dot3(p, p) for p in pairs]
    thirds = [dot3(split(q), p) for q, p in zip(seconds, pairs)]
    sums = [r + q + t for r, q, t in zip(residuals, seconds, thirds)]
    cubes = [split(t) for t in thirds]
    sixths = [dot3(c, c) + eye for c in cubes]
    quartics = [
        dot3(split(u + GOLDEN * t), split(u - (1.0 / GOLDEN) * t)) for u, t in zip(sixths, thirds)
    ]
    longs = [dot3(split(r), split(q)) for r, q in zip(sums, quartics)]
    return [
        (eye + jnp.where(f, x, r)) * s for f, x, r, s in zip(slow, longs, sums, scales)
    ]


def to_pieces(green, out_ref, base, block):
    slab = slice(block * 64, block * 64 + 64)
    for q, tiles in enumerate(transpose_rows([g[slab].reshape(8, 8, M) for g in green])):
        for t in range(8):
            for half in range(2):
                piece = base + block * 32 + 4 * t + 2 * (q // 2) + half
                rows = slice(q % 2 * 8, q % 2 * 8 + 8)
                out_ref[piece, rows] = tiles[t, :, half * 128 : half * 128 + 128]


def solve_kernel(
    sigma_hbm,
    ham_hbm,
    coup_hbm,
    energy_hbm,
    count_hbm,
    out_ref,
    sigma_ref,
    ham_ref,
    coup_ref,
    energy_ref,
    count_ref,
    sems,
):
    upper, lower = pl.ds(0, M), pl.ds(M, M)
    copies = [
        pltpu.make_async_copy(coup_hbm, coup_ref, sems.at[0]),
        pltpu.make_async_copy(ham_hbm.at[upper], ham_ref.at[upper], sems.at[1]),
        *(
            pltpu.make_async_copy(sigma_hbm.at[p, upper], sigma_ref.at[p, upper], sems.at[2 + p])
            for p in range(PTS)
        ),
        pltpu.make_async_copy(ham_hbm.at[lower], ham_ref.at[lower], sems.at[6]),
        pltpu.make_async_copy(sigma_hbm.at[:, lower], sigma_ref.at[:, lower], sems.at[7]),
    ]
    scalars = [
        pltpu.make_async_copy(energy_hbm, energy_ref, sems.at[16]),
        pltpu.make_async_copy(count_hbm, count_ref, sems.at[17]),
    ]
    for copy in scalars:
        copy.start()
    for copy in copies[1:6] + copies[:1] + copies[6:]:
        copy.start()
    for copy in scalars:
        copy.wait()
    rank = (lax.axis_index("xl") * 8 + lax.axis_index("z")) * 2 + lax.axis_index("c")
    points = range(PTS)
    energy = [energy_ref[rank * PTS + p] for p in points]
    slow = [count_ref[rank * PTS + p] > 2 for p in points]
    scale = [1.0 / jnp.full((1, 1), e, F32) for e in energy]
    copies[1].wait()
    residual = []
    for p in points:
        copies[2 + p].wait()
        residual.append((ham_ref[:M] + sigma_ref[p, :M]) * scale[p])
    left = invert_all(residual, scale, slow)
    for copy in copies[6:]:
        copy.wait()
    copies[0].wait()
    coupling = split(coup_ref[...])
    turned = split(coup_ref[...].T)
    inverse = [split(x) for x in left]
    coupled = [split(dot3(x, coupling)) for x in inverse]
    back = [split(dot3(turned, x)) for x in inverse]
    residual = [
        (ham_ref[M:] + sigma_ref[p, M:] + dot3(turned, coupled[p])) * scale[p] for p in points
    ]
    right = invert_all(residual, scale, slow)
    through = [split(dot3(c, split(r))) for c, r in zip(coupled, right)]
    for base, green in ((128, right), (0, None)):
        if green is None:
            green = [x + dot3(t, b) for x, t, b in zip(left, through, back)]
        for block in range(4):
            to_pieces(green, out_ref, base, block)


def solve(sigma, ham, coupling, energies, counts):
    hbm = pl.BlockSpec(memory_space=pltpu.HBM)
    sigma, ham, coupling, energies, counts = (
        pltpu.with_memory_space_constraint(v, pltpu.HBM) for v in (sigma, ham, coupling, energies, counts)
    )
    return pl.pallas_call(
        solve_kernel,
        out_shape=jax.ShapeDtypeStruct((DEVS, ROWS, 128), F32),
        in_specs=[hbm] * 5,
        out_specs=vmem(),
        scratch_shapes=[
            pltpu.VMEM((PTS, 2 * M, M), F32),
            pltpu.VMEM((2 * M, M), F32),
            pltpu.VMEM((M, M), F32),
            pltpu.SMEM((E_TOT,), F32),
            pltpu.SMEM((E_TOT,), jnp.int32),
            pltpu.SemaphoreType.DMA((18,)),
        ],
        compiler_params=pltpu.CompilerParams(vmem_limit_bytes=40 * 1024 * 1024),
        cost_estimate=pl.CostEstimate(flops=6_800_000_000, bytes_accessed=5_000_000, transcendentals=0),
        name="solve_points",
    )(sigma, ham, coupling, energies, counts)


def lorentz(offset):
    scaled = offset / BROADENING
    return 1.0 / (1.0 + scaled * scaled)


def energy_operator(energies):
    columns = jnp.broadcast_to(energies, (E_TOT, E_TOT))
    spacing = columns.T - columns
    values = lorentz(spacing - PHONON) + lorentz(spacing + PHONON)
    values = values / jnp.sum(values, axis=1, keepdims=True)
    wide = E_TOT * 2
    spread = (
        lax.broadcasted_iota(jnp.int32, (wide, E_TOT), 0) // 2
        == lax.broadcasted_iota(jnp.int32, (wide, E_TOT), 1)
    ).astype(BF16)
    gather = (
        lax.broadcasted_iota(jnp.int32, (E_TOT, wide), 1) // 2
        == lax.broadcasted_iota(jnp.int32, (E_TOT, wide), 0)
    ).astype(BF16)
    row_id = lax.broadcasted_iota(jnp.int32, (wide, wide), 0)
    col_id = lax.broadcasted_iota(jnp.int32, (wide, wide), 1)
    same = ((row_id ^ col_id) & 1) == 0
    parts = []
    for part in split(values):
        tall = jnp.dot(spread, part, preferred_element_type=F32).astype(BF16)
        full = jnp.dot(tall, gather, preferred_element_type=F32)
        parts.append(jnp.where(same, full, 0.0).astype(BF16))
    return parts


def cyclic_four(a, weight):
    even, odd, even_change, odd_change = weight
    sums = a[0] + a[2], a[1] + a[3]
    gaps = a[0] - a[2], a[1] - a[3]
    cyclic = even * sums[0] + odd * sums[1], even * sums[1] + odd * sums[0]
    signed = (
        even_change * gaps[0] - odd_change * gaps[1],
        even_change * gaps[1] + odd_change * gaps[0],
    )
    return [cyclic[0] + signed[0], cyclic[1] + signed[1], cyclic[0] - signed[0], cyclic[1] - signed[1]]


def mix_momenta(given, weight):
    half = KN // 2
    total, change = weight
    added = [given[k] + given[k + half] for k in range(half)]
    taken = [given[k] - given[k + half] for k in range(half)]
    first, second = [], []
    cycles = cyclic_four(added, total)
    for k in range(half):
        cyclic = cycles[k]
        signed = change[0] * taken[k]
        for s in range(1, half):
            term = change[s] * taken[(k - s) % half]
            signed = signed + term if k >= s else signed - term
        first.append(cyclic + signed)
        second.append(cyclic - signed)
    return first + second


def mix_kernel(energy_ref, strength_ref, offset_ref, in_ref, out_ref, x_high, x_low):
    weight = []
    for d in range(KN):
        chosen = jnp.where(offset_ref[...] == d, strength_ref[...], 0.0)
        weight.append(jnp.sum(chosen, axis=1, keepdims=True))
    half = KN // 2
    total = [0.5 * (weight[s] + weight[s + half]) for s in range(half)]
    change = [0.5 * (weight[s] - weight[s + half]) for s in range(half)]
    total = [0.5 * (total[s] + sign * total[s + 2]) for sign in (1.0, -1.0) for s in range(2)]
    halves = [[jnp.broadcast_to(w, (ROWS, 128)) for w in part] for part in (total, change)]
    high, low = energy_operator(energy_ref[...])
    left = jnp.concatenate([high, high, low], axis=1)
    for upper in range(2):
        for device in range(16):
            given = [in_ref[(upper * KN + k) * 16 + device] for k in range(KN)]
            rows = slice((upper * 16 + device) * 8, (upper * 16 + device) * 8 + 8)
            for k, mixed in enumerate(mix_momenta(given, halves)):
                for tile, part in enumerate(split(mixed)):
                    ref = (x_high, x_low)[tile]
                    ref[rows, k * 256 : k * 256 + 128] = part[:8]
                    ref[rows, k * 256 + 128 : k * 256 + 256] = part[8:]
    for k in range(KN):
        lanes = slice(k * 256, k * 256 + 256)
        right = jnp.concatenate([x_high[:, lanes], x_low[:, lanes], x_high[:, lanes]], axis=0)
        mixed = jnp.dot(left, right, preferred_element_type=F32).reshape(32, 8, 256)
        for upper in range(2):
            part = mixed[upper * 16 : upper * 16 + 16]
            first = (upper * KN + k) * 16
            out_ref[first : first + 16, :8] = part[:, :, :128]
            out_ref[first : first + 16, 8:] = part[:, :, 128:]


def mix(energies, strengths, offsets, x):
    return pl.pallas_call(
        mix_kernel,
        out_shape=jax.ShapeDtypeStruct((DEVS, ROWS, 128), F32),
        in_specs=[vmem()] * 4,
        out_specs=vmem(),
        scratch_shapes=[
            pltpu.VMEM((256, 2048), BF16),
            pltpu.VMEM((256, 2048), BF16),
        ],
        compiler_params=pltpu.CompilerParams(vmem_limit_bytes=32 * 1024 * 1024),
        cost_estimate=pl.CostEstimate(flops=900_000_000, bytes_accessed=4_200_000, transcendentals=0),
        name="mix_energies",
    )(energies, strengths, offsets, x)


def blend_kernel(sigma_ref, in_ref, out_hbm, out_ref, sems):
    copies = []
    for block in range(8):
        for t in range(8 * block, 8 * block + 8):
            rows = slice(8 * t, 8 * t + 8)
            for half in range(2):
                lanes = slice(half * 128, half * 128 + 128)
                even = in_ref[4 * t + half]
                odd = in_ref[4 * t + 2 + half]
                tiles = transpose_rows((even[:8], even[8:], odd[:8], odd[8:]))
                for p, tile in enumerate(tiles):
                    old = sigma_ref[p, rows, lanes]
                    out_ref[p, rows, lanes] = (1.0 - MIX_RATE) * old + MIX_RATE * tile
        rows = pl.ds(64 * block, 64)
        copies.append(
            pltpu.make_async_copy(out_ref.at[:, rows], out_hbm.at[:, rows], sems.at[block])
        )
        copies[-1].start()
    for copy in copies:
        copy.wait()


def blend(sigma, x):
    return pl.pallas_call(
        blend_kernel,
        out_shape=jax.ShapeDtypeStruct((PTS, 2 * M, M), F32),
        in_specs=[vmem(), vmem()],
        out_specs=pl.BlockSpec(memory_space=pltpu.HBM),
        scratch_shapes=[pltpu.VMEM((PTS, 2 * M, M), F32), pltpu.SemaphoreType.DMA((8,))],
        compiler_params=pltpu.CompilerParams(vmem_limit_bytes=24 * 1024 * 1024),
        cost_estimate=pl.CostEstimate(flops=2_000_000, bytes_accessed=6_000_000, transcendentals=0),
        name="blend_old",
    )(sigma, x)


def exchange(x):
    return lax.all_to_all(x, ORDER, split_axis=0, concat_axis=0, tiled=True)


def body(sigma_in, hamiltonian, coupling, energies, counts, strengths, offsets):
    sigma = sigma_in.reshape(PTS, 2 * M, M)
    green = solve(sigma, hamiltonian.reshape(2 * M, M), coupling.reshape(M, M), energies, counts)
    columns = exchange(green)
    mixed = mix(energies.reshape(1, -1), strengths.reshape(1, -1), offsets.reshape(1, -1), columns)
    result = exchange(mixed)
    return blend(sigma, result).reshape(sigma_in.shape)


def solution(mesh):
    fine = Mesh(mesh.devices.reshape(2, 8, 2, 2, 4), ("xl", "z", "c", "xh", "y"))
    energy, mom = ("xl", "z", "c"), ("xh", "y")
    return jax.shard_map(
        body,
        mesh=fine,
        in_specs=(
            P(energy, mom, None, None, None),
            P(mom, None, None, None),
            P(mom, None, None),
            P(),
            P(),
            P(),
            P(),
        ),
        out_specs=P(energy, mom, None, None, None),
        check_vma=False,
    )
```

```python
import jax
import jax.numpy as jnp
from jax import lax
from jax.experimental import pallas as pl
from jax.experimental.pallas import tpu as pltpu
from jax.sharding import Mesh
from jax.sharding import PartitionSpec as P

MIX_RATE = 0.6
PHONON = 0.1
BROADENING = 0.02
GOLDEN = 0.5 + 0.5 * 5.0**0.5

M = 256
PTS = 4
E_TOT = 128
KN = 8
DEVS = 256
ROWS = 16
ORDER = ("xl", "xh", "y", "z", "c")
F32 = jnp.float32
BF16 = jnp.bfloat16


def vmem():
    return pl.BlockSpec(memory_space=pltpu.VMEM)


def split(x):
    high = x.astype(BF16)
    return high, (x - high.astype(F32)).astype(BF16)


def dot3(a, b):
    stacked = jnp.dot(jnp.concatenate(a, axis=0), b[0], preferred_element_type=F32)
    return stacked[:M] + (stacked[M:] + jnp.dot(a[0], b[1], preferred_element_type=F32))


def exchange_rows(x, y, group):
    axis = x.ndim - 2
    even = lax.broadcasted_iota(jnp.int32, x.shape, axis) // group % 2 == 0
    first = jnp.where(even, x, pltpu.roll(y, group, axis))
    second = jnp.where(even, pltpu.roll(x, 8 - group, axis), y)
    return first, second


def transpose_rows(tiles):
    a, c = exchange_rows(tiles[0], tiles[2], 4)
    b, d = exchange_rows(tiles[1], tiles[3], 4)
    return exchange_rows(a, b, 2) + exchange_rows(c, d, 2)


def invert_all(residuals, scales, slow):
    rows = lax.broadcasted_iota(jnp.int32, (M, M), 0)
    cols = lax.broadcasted_iota(jnp.int32, (M, M), 1)
    eye = (rows == cols).astype(F32)
    pairs = [split(r) for r in residuals]
    seconds = [dot3(p, p) for p in pairs]
    thirds = [dot3(split(q), p) for q, p in zip(seconds, pairs)]
    sums = [r + q + t for r, q, t in zip(residuals, seconds, thirds)]
    cubes = [split(t) for t in thirds]
    sixths = [dot3(c, c) + eye for c in cubes]
    quartics = [
        dot3(split(u + GOLDEN * t), split(u - (1.0 / GOLDEN) * t)) for u, t in zip(sixths, thirds)
    ]
    longs = [dot3(split(r), split(q)) for r, q in zip(sums, quartics)]
    return [
        (eye + jnp.where(f, x, r)) * s for f, x, r, s in zip(slow, longs, sums, scales)
    ]


def to_pieces(green, out_ref, base, block):
    slab = slice(block * 64, block * 64 + 64)
    for q, tiles in enumerate(transpose_rows([g[slab].reshape(8, 8, M) for g in green])):
        for t in range(8):
            for half in range(2):
                piece = base + block * 32 + 4 * t + 2 * (q // 2) + half
                rows = slice(q % 2 * 8, q % 2 * 8 + 8)
                out_ref[piece, rows] = tiles[t, :, half * 128 : half * 128 + 128]


def solve_kernel(
    sigma_hbm,
    ham_hbm,
    coup_hbm,
    energy_hbm,
    count_hbm,
    out_ref,
    sigma_ref,
    ham_ref,
    coup_ref,
    energy_ref,
    count_ref,
    sems,
):
    upper, lower = pl.ds(0, M), pl.ds(M, M)
    copies = [
        pltpu.make_async_copy(coup_hbm, coup_ref, sems.at[0]),
        pltpu.make_async_copy(ham_hbm.at[upper], ham_ref.at[upper], sems.at[1]),
        *(
            pltpu.make_async_copy(sigma_hbm.at[p, upper], sigma_ref.at[p, upper], sems.at[2 + p])
            for p in range(PTS)
        ),
        pltpu.make_async_copy(ham_hbm.at[lower], ham_ref.at[lower], sems.at[6]),
        pltpu.make_async_copy(sigma_hbm.at[:, lower], sigma_ref.at[:, lower], sems.at[7]),
    ]
    scalars = [
        pltpu.make_async_copy(energy_hbm, energy_ref, sems.at[16]),
        pltpu.make_async_copy(count_hbm, count_ref, sems.at[17]),
    ]
    for copy in scalars:
        copy.start()
    for copy in copies[1:6] + copies[:1] + copies[6:]:
        copy.start()
    for copy in scalars:
        copy.wait()
    rank = (lax.axis_index("xl") * 8 + lax.axis_index("z")) * 2 + lax.axis_index("c")
    points = range(PTS)
    energy = [energy_ref[rank * PTS + p] for p in points]
    slow = [count_ref[rank * PTS + p] > 2 for p in points]
    scale = [1.0 / jnp.full((1, 1), e, F32) for e in energy]
    copies[1].wait()
    residual = []
    for p in points:
        copies[2 + p].wait()
        residual.append((ham_ref[:M] + sigma_ref[p, :M]) * scale[p])
    left = invert_all(residual, scale, slow)
    for copy in copies[6:]:
        copy.wait()
    copies[0].wait()
    coupling = split(coup_ref[...])
    turned = split(coup_ref[...].T)
    inverse = [split(x) for x in left]
    coupled = [split(dot3(x, coupling)) for x in inverse]
    back = [split(dot3(turned, x)) for x in inverse]
    residual = [
        (ham_ref[M:] + sigma_ref[p, M:] + dot3(turned, coupled[p])) * scale[p] for p in points
    ]
    right = invert_all(residual, scale, slow)
    through = [split(dot3(c, split(r))) for c, r in zip(coupled, right)]
    for base, green in ((128, right), (0, None)):
        if green is None:
            green = [x + dot3(t, b) for x, t, b in zip(left, through, back)]
        for block in range(4):
            to_pieces(green, out_ref, base, block)


def solve(sigma, ham, coupling, energies, counts):
    hbm = pl.BlockSpec(memory_space=pltpu.HBM)
    sigma, ham, coupling, energies, counts = (
        pltpu.with_memory_space_constraint(v, pltpu.HBM) for v in (sigma, ham, coupling, energies, counts)
    )
    return pl.pallas_call(
        solve_kernel,
        out_shape=jax.ShapeDtypeStruct((DEVS, ROWS, 128), F32),
        in_specs=[hbm] * 5,
        out_specs=vmem(),
        scratch_shapes=[
            pltpu.VMEM((PTS, 2 * M, M), F32),
            pltpu.VMEM((2 * M, M), F32),
            pltpu.VMEM((M, M), F32),
            pltpu.SMEM((E_TOT,), F32),
            pltpu.SMEM((E_TOT,), jnp.int32),
            pltpu.SemaphoreType.DMA((18,)),
        ],
        compiler_params=pltpu.CompilerParams(vmem_limit_bytes=40 * 1024 * 1024),
        cost_estimate=pl.CostEstimate(flops=6_800_000_000, bytes_accessed=5_000_000, transcendentals=0),
        name="solve_points",
    )(sigma, ham, coupling, energies, counts)


def lorentz(offset):
    scaled = offset / BROADENING
    return 1.0 / (1.0 + scaled * scaled)


def energy_operator(energies):
    columns = jnp.broadcast_to(energies, (E_TOT, E_TOT))
    spacing = columns.T - columns
    values = lorentz(spacing - PHONON) + lorentz(spacing + PHONON)
    values = values / jnp.sum(values, axis=1, keepdims=True)
    wide = E_TOT * 2
    spread = (
        lax.broadcasted_iota(jnp.int32, (wide, E_TOT), 0) // 2
        == lax.broadcasted_iota(jnp.int32, (wide, E_TOT), 1)
    ).astype(BF16)
    gather = (
        lax.broadcasted_iota(jnp.int32, (E_TOT, wide), 1) // 2
        == lax.broadcasted_iota(jnp.int32, (E_TOT, wide), 0)
    ).astype(BF16)
    row_id = lax.broadcasted_iota(jnp.int32, (wide, wide), 0)
    col_id = lax.broadcasted_iota(jnp.int32, (wide, wide), 1)
    same = ((row_id ^ col_id) & 1) == 0
    parts = []
    for part in split(values):
        tall = jnp.dot(spread, part, preferred_element_type=F32).astype(BF16)
        full = jnp.dot(tall, gather, preferred_element_type=F32)
        parts.append(jnp.where(same, full, 0.0).astype(BF16))
    return parts


def cyclic_four(a, weight):
    even, odd, even_change, odd_change = weight
    sums = a[0] + a[2], a[1] + a[3]
    gaps = a[0] - a[2], a[1] - a[3]
    cyclic = even * sums[0] + odd * sums[1], even * sums[1] + odd * sums[0]
    signed = (
        even_change * gaps[0] - odd_change * gaps[1],
        even_change * gaps[1] + odd_change * gaps[0],
    )
    return [cyclic[0] + signed[0], cyclic[1] + signed[1], cyclic[0] - signed[0], cyclic[1] - signed[1]]


def mix_momenta(given, weight):
    half = KN // 2
    total, change = weight
    added = [given[k] + given[k + half] for k in range(half)]
    taken = [given[k] - given[k + half] for k in range(half)]
    first, second = [], []
    cycles = cyclic_four(added, total)
    for k in range(half):
        cyclic = cycles[k]
        signed = change[0] * taken[k]
        for s in range(1, half):
            term = change[s] * taken[(k - s) % half]
            signed = signed + term if k >= s else signed - term
        first.append(cyclic + signed)
        second.append(cyclic - signed)
    return first + second


def mix_kernel(energy_ref, strength_ref, offset_ref, in_ref, out_ref, x_high, x_low):
    weight = []
    for d in range(KN):
        chosen = jnp.where(offset_ref[...] == d, strength_ref[...], 0.0)
        weight.append(jnp.sum(chosen, axis=1, keepdims=True))
    half = KN // 2
    total = [0.5 * (weight[s] + weight[s + half]) for s in range(half)]
    change = [0.5 * (weight[s] - weight[s + half]) for s in range(half)]
    total = [0.5 * (total[s] + sign * total[s + 2]) for sign in (1.0, -1.0) for s in range(2)]
    halves = [[jnp.broadcast_to(w, (ROWS, 128)) for w in part] for part in (total, change)]
    high, low = energy_operator(energy_ref[...])
    left = jnp.concatenate([high, high, low], axis=1)
    for upper in range(2):
        for device in range(16):
            given = [in_ref[(upper * KN + k) * 16 + device] for k in range(KN)]
            rows = slice((upper * 16 + device) * 8, (upper * 16 + device) * 8 + 8)
            for k, mixed in enumerate(mix_momenta(given, halves)):
                for tile, part in enumerate(split(mixed)):
                    ref = (x_high, x_low)[tile]
                    ref[rows, k * 256 : k * 256 + 128] = part[:8]
                    ref[rows, k * 256 + 128 : k * 256 + 256] = part[8:]
    for k in range(KN):
        lanes = slice(k * 256, k * 256 + 256)
        right = jnp.concatenate([x_high[:, lanes], x_low[:, lanes], x_high[:, lanes]], axis=0)
        mixed = jnp.dot(left, right, preferred_element_type=F32).reshape(32, 8, 256)
        for upper in range(2):
            part = mixed[upper * 16 : upper * 16 + 16]
            first = (upper * KN + k) * 16
            out_ref[first : first + 16, :8] = part[:, :, :128]
            out_ref[first : first + 16, 8:] = part[:, :, 128:]


def mix(energies, strengths, offsets, x):
    return pl.pallas_call(
        mix_kernel,
        out_shape=jax.ShapeDtypeStruct((DEVS, ROWS, 128), F32),
        in_specs=[vmem()] * 4,
        out_specs=vmem(),
        scratch_shapes=[
            pltpu.VMEM((256, 2048), BF16),
            pltpu.VMEM((256, 2048), BF16),
        ],
        compiler_params=pltpu.CompilerParams(vmem_limit_bytes=32 * 1024 * 1024),
        cost_estimate=pl.CostEstimate(flops=900_000_000, bytes_accessed=4_200_000, transcendentals=0),
        name="mix_energies",
    )(energies, strengths, offsets, x)


def blend_kernel(sigma_ref, in_ref, out_hbm, out_ref, sems):
    copies = []
    for block in range(8):
        for t in range(8 * block, 8 * block + 8):
            rows = slice(8 * t, 8 * t + 8)
            for half in range(2):
                lanes = slice(half * 128, half * 128 + 128)
                even = in_ref[4 * t + half]
                odd = in_ref[4 * t + 2 + half]
                tiles = transpose_rows((even[:8], even[8:], odd[:8], odd[8:]))
                for p, tile in enumerate(tiles):
                    old = sigma_ref[p, rows, lanes]
                    out_ref[p, rows, lanes] = (1.0 - MIX_RATE) * old + MIX_RATE * tile
        rows = pl.ds(64 * block, 64)
        copies.append(
            pltpu.make_async_copy(out_ref.at[:, rows], out_hbm.at[:, rows], sems.at[block])
        )
        copies[-1].start()
    for copy in copies:
        copy.wait()


def blend(sigma, x):
    return pl.pallas_call(
        blend_kernel,
        out_shape=jax.ShapeDtypeStruct((PTS, 2 * M, M), F32),
        in_specs=[vmem(), vmem()],
        out_specs=pl.BlockSpec(memory_space=pltpu.HBM),
        scratch_shapes=[pltpu.VMEM((PTS, 2 * M, M), F32), pltpu.SemaphoreType.DMA((8,))],
        compiler_params=pltpu.CompilerParams(vmem_limit_bytes=24 * 1024 * 1024),
        cost_estimate=pl.CostEstimate(flops=2_000_000, bytes_accessed=6_000_000, transcendentals=0),
        name="blend_old",
    )(sigma, x)


def exchange(x):
    return lax.all_to_all(x, ORDER, split_axis=0, concat_axis=0, tiled=True)


def body(sigma_in, hamiltonian, coupling, energies, counts, strengths, offsets):
    sigma = sigma_in.reshape(PTS, 2 * M, M)
    green = solve(sigma, hamiltonian.reshape(2 * M, M), coupling.reshape(M, M), energies, counts)
    columns = exchange(green)
    mixed = mix(energies.reshape(1, -1), strengths.reshape(1, -1), offsets.reshape(1, -1), columns)
    result = exchange(mixed)
    return blend(sigma, result).reshape(sigma_in.shape)


def solution(mesh):
    fine = Mesh(mesh.devices.reshape(2, 8, 2, 2, 4), ("xl", "z", "c", "xh", "y"))
    energy, mom = ("xl", "z", "c"), ("xh", "y")
    return jax.shard_map(
        body,
        mesh=fine,
        in_specs=(
            P(energy, mom, None, None, None),
            P(mom, None, None, None),
            P(mom, None, None),
            P(),
            P(),
            P(),
            P(),
        ),
        out_specs=P(energy, mom, None, None, None),
        check_vma=False,
    )
```
